256 devices in a mesh: row: 16 (over y, x), col: 16 (over z, core).
Axes of the slice: x: 4, y: 4, z: 8, core: 2. Of those that a mesh axis runs over, the one named last changes fastest.
Arguments:
- matrix: float32 [16384, 4, 4096], P('row', None, 'col'), may hold values from -28 to 28
Outputs:
- coefficients: float32 [512, 4, 4096], P(None, None, 'col')
- remainder: float32 [16384, 4, 4096], P('row', None, 'col')
The draws below stay inside these ranges and needn't reach their ends.
All inputs are finite; a program needn't handle non-finite values.
Results may differ from the reference program's by a relative error of at most 0.0003.
Values sent between devices are 32-bit elements; how exact they have to be, the bound alone decides.
No kernel may reach another device: no remote copies, remote signals or barrier semaphores. Data moves between devices by JAX's collectives and lax.ppermute only.
A program may use at most 64 MiB of HBM per device.

```python
import jax
import jax.numpy as jnp
from jax import lax

BLOCK = 256
NBL = 4
ROWS = 16384
SPAN = 4096


def draw_matrix(key, part):
    first = jax.random.fold_in(key, 0)
    shape = (ROWS, NBL, SPAN)
    return jax.random.truncated_normal(first, -4.0, 4.0, shape, jnp.float32)


def setup_inputs(seed: int = 0) -> dict:
    keys = jax.random.split(jax.random.key(seed), 2)
    matrix = draw_matrix(jax.random.fold_in(keys[1], 71), 0)
    return {"matrix": matrix}


def reference(matrix):
    total_rows = matrix.shape[0]
    flat = matrix.reshape(total_rows, -1)
    panel = flat[:, :2 * BLOCK]
    factor, upper = jnp.linalg.qr(panel)
    signs = jnp.sign(jnp.diagonal(upper))
    factor = factor * signs[None, :]
    coefficients = jnp.dot(factor.T.astype(jnp.float32), flat.astype(jnp.float32), precision=lax.Precision.HIGHEST, preferred_element_type=jnp.float32)
    remainder = flat - jnp.dot(factor.astype(jnp.float32), coefficients.astype(jnp.float32), precision=lax.Precision.HIGHEST, preferred_element_type=jnp.float32)
    return (coefficients.reshape(2 * BLOCK, NBL, SPAN), remainder.reshape(matrix.shape))
```

```python
import jax
import jax.numpy as jnp
from jax import lax
from jax.experimental import pallas as pl
from jax.experimental.pallas import tpu as pltpu
from jax.sharding import PartitionSpec as P

BLOCK = 256
TILE = 128
NB = 4
STRIP = 4
FULL = NB * TILE
PEERS = 16
DEPTH = 8
PIECE = 128
SHARE = FULL // PEERS
HALF = ((0, 0), (1, 0), (1, 1), (2, 0), (2, 1)), ((2, 2), (3, 0), (3, 1), (3, 2), (3, 3))
HALF_ROWS = len(HALF[0]) * TILE

highest = lax.Precision.HIGHEST
by_rows = ((0,), (0,))
plain = ((1,), (0,))
by_cols = ((1,), (1,))


def mm(a, b, dims):
    return lax.dot_general(a, b, (dims, ((), ())), precision=highest, preferred_element_type=jnp.float32)

def invert_factor(s):
    n = TILE
    rows = lax.broadcasted_iota(jnp.int32, (n, n), 0)
    cols = lax.broadcasted_iota(jnp.int32, (n, n), 1)
    t = jnp.where(rows == cols, 1.0, 0.0).astype(jnp.float32)
    s_done, t_done = [], []
    for k in range(0, n, STRIP):
        top = (k // 8) * 8
        off = k - top
        height = n - top
        sub = lax.broadcasted_iota(jnp.int32, (height, n), 0)
        col = [jnp.broadcast_to(s[:, k + m : k + m + 1], (height, n)) for m in range(STRIP)]
        pivot = [[jnp.broadcast_to(col[j][off + i : off + i + 1, :], (8, n)) for j in range(STRIP)] for i in range(STRIP)]
        srow = [jnp.broadcast_to(s[off + m : off + m + 1, :], (8, n)) for m in range(STRIP)]
        trow = [jnp.broadcast_to(t[off + m : off + m + 1, :], (8, n)) for m in range(STRIP)]
        inv = []
        for m in range(STRIP):
            inv.append(1.0 / pivot[m][m])
            for i in range(m + 1, STRIP):
                low = pivot[i][m] * inv[m]
                for j in range(m + 1, STRIP):
                    if j <= i:
                        pivot[i][j] = pivot[i][j] - low * pivot[j][m]
                srow[i] = srow[i] - low * srow[m]
                trow[i] = trow[i] - low * trow[m]
        def tall(x):
            return jnp.concatenate([x] * (height // 8), axis=0) if height > 8 else x
        factor = []
        for m in range(STRIP):
            f = col[m]
            for j in range(m):
                f = f - factor[j] * tall(pivot[m][j])
            f = f * tall(inv[m])
            factor.append(f)
        for m in range(STRIP):
            f = jnp.where(sub > off + m, factor[m], 0.0)
            s = s - f * tall(srow[m])
            t = t - f * tall(trow[m])
        if off + STRIP == 8:
            s_done.append(s[:8])
            t_done.append(t[:8])
            if height > 8:
                s, t = s[8:], t[8:]
    s = jnp.concatenate(s_done, axis=0)
    t = jnp.concatenate(t_done, axis=0)
    diag = jnp.sum(jnp.where(rows == cols, s, 0.0), axis=1, keepdims=True)
    return t * lax.rsqrt(diag)


def split(x):
    high = x.astype(jnp.bfloat16)
    return high, (x - high.astype(jnp.float32)).astype(jnp.bfloat16)


def one_pass(a, b, dims):
    return lax.dot_general(a, b, (dims, ((), ())), preferred_element_type=jnp.float32)


def three_pass(a, b, dims):
    return one_pass(a[0], b[0], dims) + (one_pass(a[0], b[1], dims) + one_pass(a[1], b[0], dims))


def gram_kernel(place, own_ref, other_ref, high_ref, low_ref, gram_ref):
    first = place[1] == 0
    own, other = own_ref[...], other_ref[...]
    panel = jnp.concatenate([jnp.where(first, own, other), jnp.where(first, other, own)], axis=1)
    parts = split(panel)
    high_ref[...], low_ref[...] = parts
    gram = three_pass(parts, parts, by_rows)
    for t in range(len(HALF[0])):
        (i, j), (p, q) = HALF[0][t], HALF[1][t]
        here = gram[i * TILE : (i + 1) * TILE, j * TILE : (j + 1) * TILE]
        there = gram[p * TILE : (p + 1) * TILE, q * TILE : (q + 1) * TILE]
        gram_ref[t * TILE : (t + 1) * TILE, :] = jnp.where(first, here, there)


def product_kernel(place, high_ref, low_ref, a0_ref, a1_ref, *refs):
    outs, acc_ref = refs[:-1], refs[-1]
    step = pl.program_id(0)

    @pl.when(step == 0)
    def _():
        acc_ref[...] = jnp.zeros_like(acc_ref)

    panel = high_ref[...], low_ref[...]
    for l in range(a0_ref.shape[0]):
        a = split(jnp.concatenate([a0_ref[l], a1_ref[l]], axis=0))
        acc_ref[:, l * BLOCK : (l + 1) * BLOCK] += three_pass(panel, a, by_rows)

    @pl.when(step == pl.num_programs(0) - 1)
    def _():
        for s in range(PEERS):
            chunk = lax.rem(place[2] + s, PEERS)
            outs[s][...] = acc_ref[pl.ds(pl.multiple_of(chunk * SHARE, SHARE), SHARE), :]


def factor_kernel(place, own_ref, other_ref, m_ref, s_ref, t_ref):
    first = place[1] == 0
    s_ref[...] = jnp.zeros_like(s_ref)
    t_ref[...] = jnp.zeros_like(t_ref)
    for t in range(len(HALF[0])):
        own, other = own_ref[t * TILE : (t + 1) * TILE, :], other_ref[t * TILE : (t + 1) * TILE, :]
        for (i, j), block in zip((HALF[0][t], HALF[1][t]), (jnp.where(first, own, other), jnp.where(first, other, own))):
            s_ref[j, i * TILE : (i + 1) * TILE, :] = block

    @pl.loop(0, NB)
    def _(j):
        d = pl.multiple_of(j * TILE, TILE)
        mj = invert_factor(s_ref[j, pl.ds(d, TILE), :])
        mrow = mm(mj, t_ref[j], plain)
        lanes = lax.broadcasted_iota(jnp.int32, (TILE, FULL), 1)
        mrow = jnp.where(lanes // TILE == j, jnp.concatenate([mj] * NB, axis=1), mrow)
        m_ref[pl.ds(d, TILE), :] = mrow
        rows = lax.broadcasted_iota(jnp.int32, (FULL, TILE), 0)
        low = jnp.where(rows >= d + TILE, mm(s_ref[j], mj, by_cols), 0.0)
        for i in range(1, NB):

            @pl.when(i > j)
            def _():
                part = low[i * TILE : (i + 1) * TILE]
                s_ref[i] -= mm(low, part, by_cols)
                t_ref[i] -= mm(part, mrow, plain)


def basis_kernel(place, high_ref, low_ref, m_ref, qh_ref, ql_ref):
    q = three_pass((high_ref[...], low_ref[...]), split(m_ref[...]), by_cols)
    qh_ref[...], ql_ref[...] = split(q)


def remainder_kernel(place, qh_ref, ql_ref, a_ref, m_ref, *refs):
    pieces, (coeff_ref, out_ref, w_ref, ch_ref, cl_ref) = refs[:PEERS], refs[PEERS:]
    width = a_ref.shape[2]

    @pl.when(pl.program_id(0) == 0)
    def _():
        for s in range(PEERS):
            chunk = lax.rem(place[2] + PEERS - s, PEERS)
            w_ref[pl.ds(pl.multiple_of(chunk * SHARE, SHARE), SHARE), :] = pieces[s][...]
        coeffs = three_pass(split(m_ref[...]), split(w_ref[...]), plain)
        for l in range(coeff_ref.shape[0]):
            coeff_ref[l] = coeffs[:, l * width : (l + 1) * width]
        ch_ref[...], cl_ref[...] = split(coeffs)

    q = qh_ref[...], ql_ref[...]
    for l in range(a_ref.shape[0]):
        window = slice(l * width, (l + 1) * width)
        out_ref[l] = a_ref[l] - three_pass(q, (ch_ref[:, window], cl_ref[:, window]), plain)


def call(kernel, name, grid, ins, outs, out_shape, scratch=()):
    return pl.pallas_call(
        kernel,
        out_shape=out_shape,
        grid_spec=pltpu.PrefetchScalarGridSpec(
            num_scalar_prefetch=1, grid=grid, in_specs=ins, out_specs=outs, scratch_shapes=scratch
        ),
        compiler_params=pltpu.CompilerParams(vmem_limit_bytes=44 << 20),
        name=name,
    )


def whole(*shape):
    return pl.BlockSpec(shape, lambda g, place: (0,) * len(shape))


def f32(*shape):
    return jax.ShapeDtypeStruct(shape, jnp.float32)


def bf16(*shape):
    return jax.ShapeDtypeStruct(shape, jnp.bfloat16)


def shift(x, axis, by):
    return lax.ppermute(x, axis, [(i, (i + by) % PEERS) for i in range(PEERS)])


def swap_cores(x):
    return lax.ppermute(x, "col", [(i, i ^ 1) for i in range(PEERS)])


def share_panel(mine, z):
    own = jnp.where(z == 0, mine[:PIECE], jnp.zeros((PIECE, BLOCK), jnp.float32))
    for k in range(1, DEPTH):
        own = own + lax.ppermute(mine[k * PIECE : (k + 1) * PIECE], "col", [(0, 2 * k), (1, 2 * k + 1)])
    up, down = [own], [own]
    for _ in range(DEPTH // 2 - 1):
        up.append(shift(up[-1], "col", 2))
        down.append(shift(down[-1], "col", -2))
    half = PIECE // 2
    far = [shift(up[-1][:half], "col", 2), shift(down[-1][half:], "col", -2)]
    return jnp.concatenate(down + far + up[:0:-1], axis=0)


def on_device(matrix):
    rows, blocks, width = matrix.shape
    col = lax.axis_index("col")
    z, core, row = col // 2, col % 2, lax.axis_index("row")
    place = jnp.stack([z, core, row]).astype(jnp.int32)

    own = share_panel(matrix[:, 0, :], z)
    other = swap_cores(own)
    high, low, gram = call(
        gram_kernel, "gram", (1,),
        [whole(rows, BLOCK), whole(rows, BLOCK)],
        [whole(rows, FULL), whole(rows, FULL), whole(HALF_ROWS, TILE)],
        [bf16(rows, FULL), bf16(rows, FULL), f32(HALF_ROWS, TILE)],
    )(place, own, other)

    stacked = jnp.transpose(matrix, (1, 0, 2))
    step = 2 * PIECE
    steps = rows // step
    panel_spec = pl.BlockSpec((step, FULL), lambda g, place: (g, 0))
    terms = call(
        product_kernel, "product", (steps,),
        [panel_spec, panel_spec]
        + [
            pl.BlockSpec((blocks, PIECE, width), lambda g, place, e=e: (0, lax.rem(place[0] + 2 * g + e, DEPTH), 0))
            for e in range(2)
        ],
        [whole(SHARE, blocks * width)] * PEERS,
        [f32(SHARE, blocks * width)] * PEERS,
        [pltpu.VMEM((FULL, blocks * width), jnp.float32)],
    )(place, high, low, stacked, stacked)

    gram = lax.all_to_all(gram.reshape(PEERS, HALF_ROWS // PEERS, TILE), "row", 0, 0)
    gram = jnp.broadcast_to(jnp.sum(gram, axis=0), gram.shape)
    gram = lax.all_to_all(gram, "row", 0, 0).reshape(HALF_ROWS, TILE)

    total = terms[0]
    for s in range(1, PEERS):
        total = total + shift(terms[s], "row", s)
    pieces = [total] + [shift(total, "row", s) for s in range(1, PEERS)]

    m = call(
        factor_kernel, "factor", (1,),
        [whole(HALF_ROWS, TILE)] * 2,
        whole(FULL, FULL),
        f32(FULL, FULL),
        [pltpu.VMEM((NB, FULL, TILE), jnp.float32), pltpu.VMEM((NB, TILE, FULL), jnp.float32)],
    )(place, gram, swap_cores(gram))

    rolled = pl.BlockSpec((PIECE, FULL), lambda g, place: (g, 0))
    natural = pl.BlockSpec((PIECE, FULL), lambda g, place: (lax.rem(place[0] + g, DEPTH), 0))
    qh, ql = call(
        basis_kernel, "basis", (DEPTH,),
        [rolled, rolled, whole(FULL, FULL)],
        [natural, natural],
        [bf16(rows, FULL), bf16(rows, FULL)],
    )(place, high, low, m)

    a_spec = pl.BlockSpec((blocks, step, width), lambda g, place: (0, g, 0))
    coeffs, rest = call(
        remainder_kernel, "remainder", (steps,),
        [panel_spec, panel_spec, a_spec, whole(FULL, FULL)] + [whole(SHARE, blocks * width)] * PEERS,
        [whole(blocks, FULL, width), a_spec],
        [f32(blocks, FULL, width), f32(blocks, rows, width)],
        [pltpu.VMEM((FULL, blocks * width), jnp.float32)]
        + [pltpu.VMEM((FULL, blocks * width), jnp.bfloat16)] * 2,
    )(place, qh, ql, stacked, m, *pieces)
    return jnp.transpose(coeffs, (1, 0, 2)), jnp.transpose(rest, (1, 0, 2))


def solution(mesh):
    return jax.shard_map(
        on_device,
        mesh=mesh,
        in_specs=(P("row", None, "col"),),
        out_specs=(P(None, None, "col"), P("row", None, "col")),
        check_vma=False,
    )
```

```python
import jax
import jax.numpy as jnp
from jax import lax
from jax.experimental import pallas as pl
from jax.experimental.pallas import tpu as pltpu
from jax.sharding import PartitionSpec as P

BLOCK = 256
TILE = 128
NB = 4
STRIP = 4
FULL = NB * TILE
PEERS = 16
DEPTH = 8
PIECE = 128
HALF = ((0, 0), (1, 0), (1, 1), (2, 0), (2, 1)), ((2, 2), (3, 0), (3, 1), (3, 2), (3, 3))
HALF_ROWS = len(HALF[0]) * TILE

highest = lax.Precision.HIGHEST
by_rows = ((0,), (0,))
plain = ((1,), (0,))
by_cols = ((1,), (1,))


def mm(a, b, dims):
    return lax.dot_general(a, b, (dims, ((), ())), precision=highest, preferred_element_type=jnp.float32)

def invert_factor(s):
    n = TILE
    rows = lax.broadcasted_iota(jnp.int32, (n, n), 0)
    cols = lax.broadcasted_iota(jnp.int32, (n, n), 1)
    t = jnp.where(rows == cols, 1.0, 0.0).astype(jnp.float32)
    s_done, t_done = [], []
    for k in range(0, n, STRIP):
        top = (k // 8) * 8
        off = k - top
        height = n - top
        sub = lax.broadcasted_iota(jnp.int32, (height, n), 0)
        col = [jnp.broadcast_to(s[:, k + m : k + m + 1], (height, n)) for m in range(STRIP)]
        pivot = [[jnp.broadcast_to(col[j][off + i : off + i + 1, :], (8, n)) for j in range(STRIP)] for i in range(STRIP)]
        srow = [jnp.broadcast_to(s[off + m : off + m + 1, :], (8, n)) for m in range(STRIP)]
        trow = [jnp.broadcast_to(t[off + m : off + m + 1, :], (8, n)) for m in range(STRIP)]
        inv = []
        for m in range(STRIP):
            inv.append(1.0 / pivot[m][m])
            for i in range(m + 1, STRIP):
                low = pivot[i][m] * inv[m]
                for j in range(m + 1, STRIP):
                    if j <= i:
                        pivot[i][j] = pivot[i][j] - low * pivot[j][m]
                srow[i] = srow[i] - low * srow[m]
                trow[i] = trow[i] - low * trow[m]
        def tall(x):
            return jnp.concatenate([x] * (height // 8), axis=0) if height > 8 else x
        factor = []
        for m in range(STRIP):
            f = col[m]
            for j in range(m):
                f = f - factor[j] * tall(pivot[m][j])
            f = f * tall(inv[m])
            factor.append(f)
        for m in range(STRIP):
            f = jnp.where(sub > off + m, factor[m], 0.0)
            s = s - f * tall(srow[m])
            t = t - f * tall(trow[m])
        if off + STRIP == 8:
            s_done.append(s[:8])
            t_done.append(t[:8])
            if height > 8:
                s, t = s[8:], t[8:]
    s = jnp.concatenate(s_done, axis=0)
    t = jnp.concatenate(t_done, axis=0)
    diag = jnp.sum(jnp.where(rows == cols, s, 0.0), axis=1, keepdims=True)
    return t * lax.rsqrt(diag)


def split(x):
    high = x.astype(jnp.bfloat16)
    return high, (x - high.astype(jnp.float32)).astype(jnp.bfloat16)


def one_pass(a, b, dims):
    return lax.dot_general(a, b, (dims, ((), ())), preferred_element_type=jnp.float32)


def three_pass(a, b, dims):
    return one_pass(a[0], b[0], dims) + (one_pass(a[0], b[1], dims) + one_pass(a[1], b[0], dims))


def gram_kernel(place, own_ref, other_ref, high_ref, low_ref, gram_ref):
    first = place[1] == 0
    own, other = own_ref[...], other_ref[...]
    panel = jnp.concatenate([jnp.where(first, own, other), jnp.where(first, other, own)], axis=1)
    parts = split(panel)
    high_ref[...], low_ref[...] = parts
    gram = three_pass(parts, parts, by_rows)
    for t in range(len(HALF[0])):
        (i, j), (p, q) = HALF[0][t], HALF[1][t]
        here = gram[i * TILE : (i + 1) * TILE, j * TILE : (j + 1) * TILE]
        there = gram[p * TILE : (p + 1) * TILE, q * TILE : (q + 1) * TILE]
        gram_ref[t * TILE : (t + 1) * TILE, :] = jnp.where(first, here, there)


def product_kernel(place, high_ref, low_ref, a0_ref, a1_ref, acc_ref):
    @pl.when(pl.program_id(0) == 0)
    def _():
        acc_ref[...] = jnp.zeros_like(acc_ref)

    panel = high_ref[...], low_ref[...]
    for l in range(a0_ref.shape[0]):
        a = split(jnp.concatenate([a0_ref[l], a1_ref[l]], axis=0))
        acc_ref[:, l * BLOCK : (l + 1) * BLOCK] += three_pass(panel, a, by_rows)


def factor_kernel(place, own_ref, other_ref, m_ref, s_ref, t_ref):
    first = place[1] == 0
    s_ref[...] = jnp.zeros_like(s_ref)
    t_ref[...] = jnp.zeros_like(t_ref)
    for t in range(len(HALF[0])):
        own, other = own_ref[t * TILE : (t + 1) * TILE, :], other_ref[t * TILE : (t + 1) * TILE, :]
        for (i, j), block in zip((HALF[0][t], HALF[1][t]), (jnp.where(first, own, other), jnp.where(first, other, own))):
            s_ref[j, i * TILE : (i + 1) * TILE, :] = block

    @pl.loop(0, NB)
    def _(j):
        d = pl.multiple_of(j * TILE, TILE)
        mj = invert_factor(s_ref[j, pl.ds(d, TILE), :])
        mrow = mm(mj, t_ref[j], plain)
        lanes = lax.broadcasted_iota(jnp.int32, (TILE, FULL), 1)
        mrow = jnp.where(lanes // TILE == j, jnp.concatenate([mj] * NB, axis=1), mrow)
        m_ref[pl.ds(d, TILE), :] = mrow
        rows = lax.broadcasted_iota(jnp.int32, (FULL, TILE), 0)
        low = jnp.where(rows >= d + TILE, mm(s_ref[j], mj, by_cols), 0.0)
        for i in range(1, NB):

            @pl.when(i > j)
            def _():
                part = low[i * TILE : (i + 1) * TILE]
                s_ref[i] -= mm(low, part, by_cols)
                t_ref[i] -= mm(part, mrow, plain)


def basis_kernel(place, high_ref, low_ref, m_ref, qh_ref, ql_ref):
    q = three_pass((high_ref[...], low_ref[...]), split(m_ref[...]), by_cols)
    qh_ref[...], ql_ref[...] = split(q)


def remainder_kernel(place, qh_ref, ql_ref, a_ref, m_ref, w_ref, coeff_ref, out_ref, ch_ref, cl_ref):
    width = a_ref.shape[2]

    @pl.when(pl.program_id(0) == 0)
    def _():
        coeffs = three_pass(split(m_ref[...]), split(w_ref[...]), plain)
        for l in range(coeff_ref.shape[0]):
            coeff_ref[l] = coeffs[:, l * width : (l + 1) * width]
        ch_ref[...], cl_ref[...] = split(coeffs)

    q = qh_ref[...], ql_ref[...]
    for l in range(a_ref.shape[0]):
        window = slice(l * width, (l + 1) * width)
        out_ref[l] = a_ref[l] - three_pass(q, (ch_ref[:, window], cl_ref[:, window]), plain)


def call(kernel, name, mib, grid, ins, outs, out_shape, scratch=()):
    return pl.pallas_call(
        kernel,
        out_shape=out_shape,
        grid_spec=pltpu.PrefetchScalarGridSpec(
            num_scalar_prefetch=1, grid=grid, in_specs=ins, out_specs=outs, scratch_shapes=scratch
        ),
        compiler_params=pltpu.CompilerParams(vmem_limit_bytes=mib << 20),
        name=name,
    )


def whole(*shape):
    return pl.BlockSpec(shape, lambda g, place: (0,) * len(shape))


def f32(*shape):
    return jax.ShapeDtypeStruct(shape, jnp.float32)


def bf16(*shape):
    return jax.ShapeDtypeStruct(shape, jnp.bfloat16)


def shift(x, axis, by):
    return lax.ppermute(x, axis, [(i, (i + by) % PEERS) for i in range(PEERS)])


def exchange(x):
    rows, width = x.shape
    return lax.all_to_all(x.reshape(PEERS, rows // PEERS, width), "row", 0, 0)


def everywhere(shares):
    total = jnp.broadcast_to(jnp.sum(shares, axis=0), shares.shape)
    return lax.all_to_all(total, "row", 0, 0).reshape(shares.shape[0] * shares.shape[1], shares.shape[2])


def swap_cores(x):
    return lax.ppermute(x, "col", [(i, i ^ 1) for i in range(PEERS)])


def share_panel(mine, z):
    own = jnp.where(z == 0, mine[:PIECE], jnp.zeros((PIECE, BLOCK), jnp.float32))
    for k in range(1, DEPTH):
        own = own + lax.ppermute(mine[k * PIECE : (k + 1) * PIECE], "col", [(0, 2 * k), (1, 2 * k + 1)])
    up, down = [own], [own]
    for _ in range(DEPTH // 2 - 1):
        up.append(shift(up[-1], "col", 2))
        down.append(shift(down[-1], "col", -2))
    half = PIECE // 2
    far = [shift(up[-1][:half], "col", 2), shift(down[-1][half:], "col", -2)]
    return jnp.concatenate(down + far + up[:0:-1], axis=0)


def on_device(matrix):
    rows, blocks, width = matrix.shape
    col = lax.axis_index("col")
    z, core, row = col // 2, col % 2, lax.axis_index("row")
    place = jnp.stack([z, core, row]).astype(jnp.int32)

    own = share_panel(matrix[:, 0, :], z)
    other = swap_cores(own)
    high, low, gram = call(
        gram_kernel, "gram", 20, (1,),
        [whole(rows, BLOCK), whole(rows, BLOCK)],
        [whole(rows, FULL), whole(rows, FULL), whole(HALF_ROWS, TILE)],
        [bf16(rows, FULL), bf16(rows, FULL), f32(HALF_ROWS, TILE)],
    )(place, own, other)

    stacked = jnp.transpose(matrix, (1, 0, 2))
    step = 2 * PIECE
    steps = rows // step
    panel_spec = pl.BlockSpec((step, FULL), lambda g, place: (g, 0))
    terms = call(
        product_kernel, "product", 20, (steps,),
        [panel_spec, panel_spec]
        + [
            pl.BlockSpec((blocks, PIECE, width), lambda g, place, e=e: (0, lax.rem(place[0] + 2 * g + e, DEPTH), 0))
            for e in range(2)
        ],
        whole(FULL, blocks * width),
        f32(FULL, blocks * width),
    )(place, high, low, stacked, stacked)

    gram = exchange(gram)
    terms = exchange(terms)
    gram = everywhere(gram)
    sums = everywhere(terms)

    m = call(
        factor_kernel, "factor", 12, (1,),
        [whole(HALF_ROWS, TILE)] * 2,
        whole(FULL, FULL),
        f32(FULL, FULL),
        [pltpu.VMEM((NB, FULL, TILE), jnp.float32), pltpu.VMEM((NB, TILE, FULL), jnp.float32)],
    )(place, gram, swap_cores(gram))

    rolled = pl.BlockSpec((PIECE, FULL), lambda g, place: (g, 0))
    natural = pl.BlockSpec((PIECE, FULL), lambda g, place: (lax.rem(place[0] + g, DEPTH), 0))
    qh, ql = call(
        basis_kernel, "basis", 14, (DEPTH,),
        [rolled, rolled, whole(FULL, FULL)],
        [natural, natural],
        [bf16(rows, FULL), bf16(rows, FULL)],
    )(place, high, low, m)

    a_spec = pl.BlockSpec((blocks, step, width), lambda g, place: (0, g, 0))
    coeffs, rest = call(
        remainder_kernel, "remainder", 22, (steps,),
        [panel_spec, panel_spec, a_spec, whole(FULL, FULL), whole(FULL, blocks * width)],
        [whole(blocks, FULL, width), a_spec],
        [f32(blocks, FULL, width), f32(blocks, rows, width)],
        [pltpu.VMEM((FULL, blocks * width), jnp.bfloat16)] * 2,
    )(place, qh, ql, stacked, m, sums)
    return jnp.transpose(coeffs, (1, 0, 2)), jnp.transpose(rest, (1, 0, 2))


def solution(mesh):
    return jax.shard_map(
        on_device,
        mesh=mesh,
        in_specs=(P("row", None, "col"),),
        out_specs=(P(None, None, "col"), P("row", None, "col")),
        check_vma=False,
    )
```

```python
import jax
import jax.numpy as jnp
from jax import lax
from jax.experimental import pallas as pl
from jax.experimental.pallas import tpu as pltpu
from jax.sharding import PartitionSpec as P

BLOCK = 256
TILE = 128
NB = 4
STRIP = 4
FULL = NB * TILE
PEERS = 16
DEPTH = 8
PIECE = 128
HALF = ((0, 0), (1, 0), (1, 1), (2, 0), (2, 1)), ((2, 2), (3, 0), (3, 1), (3, 2), (3, 3))
HALF_ROWS = len(HALF[0]) * TILE
SHARE = FULL // PEERS
TILES = HALF_ROWS // 8 // PEERS

highest = lax.Precision.HIGHEST
by_rows = ((0,), (0,))
plain = ((1,), (0,))
by_cols = ((1,), (1,))


def mm(a, b, dims):
    return lax.dot_general(a, b, (dims, ((), ())), precision=highest, preferred_element_type=jnp.float32)

def invert_factor(s):
    n = TILE
    rows = lax.broadcasted_iota(jnp.int32, (n, n), 0)
    cols = lax.broadcasted_iota(jnp.int32, (n, n), 1)
    t = jnp.where(rows == cols, 1.0, 0.0).astype(jnp.float32)
    s_done, t_done = [], []
    for k in range(0, n, STRIP):
        top = (k // 8) * 8
        off = k - top
        height = n - top
        sub = lax.broadcasted_iota(jnp.int32, (height, n), 0)
        col = [jnp.broadcast_to(s[:, k + m : k + m + 1], (height, n)) for m in range(STRIP)]
        pivot = [[jnp.broadcast_to(col[j][off + i : off + i + 1, :], (8, n)) for j in range(STRIP)] for i in range(STRIP)]
        srow = [jnp.broadcast_to(s[off + m : off + m + 1, :], (8, n)) for m in range(STRIP)]
        trow = [jnp.broadcast_to(t[off + m : off + m + 1, :], (8, n)) for m in range(STRIP)]
        inv = []
        for m in range(STRIP):
            inv.append(1.0 / pivot[m][m])
            for i in range(m + 1, STRIP):
                low = pivot[i][m] * inv[m]
                for j in range(m + 1, STRIP):
                    if j <= i:
                        pivot[i][j] = pivot[i][j] - low * pivot[j][m]
                srow[i] = srow[i] - low * srow[m]
                trow[i] = trow[i] - low * trow[m]
        def tall(x):
            return jnp.concatenate([x] * (height // 8), axis=0) if height > 8 else x
        factor = []
        for m in range(STRIP):
            f = col[m]
            for j in range(m):
                f = f - factor[j] * tall(pivot[m][j])
            f = f * tall(inv[m])
            factor.append(f)
        for m in range(STRIP):
            f = jnp.where(sub > off + m, factor[m], 0.0)
            s = s - f * tall(srow[m])
            t = t - f * tall(trow[m])
        if off + STRIP == 8:
            s_done.append(s[:8])
            t_done.append(t[:8])
            if height > 8:
                s, t = s[8:], t[8:]
    s = jnp.concatenate(s_done, axis=0)
    t = jnp.concatenate(t_done, axis=0)
    diag = jnp.sum(jnp.where(rows == cols, s, 0.0), axis=1, keepdims=True)
    return t * lax.rsqrt(diag)


def split(x):
    high = x.astype(jnp.bfloat16)
    return high, (x - high.astype(jnp.float32)).astype(jnp.bfloat16)


def one_pass(a, b, dims):
    return lax.dot_general(a, b, (dims, ((), ())), preferred_element_type=jnp.float32)


def three_pass(a, b, dims):
    return one_pass(a[0], b[0], dims) + (one_pass(a[0], b[1], dims) + one_pass(a[1], b[0], dims))


def panel_kernel(matrix_ref, out_ref, sem):
    copy = pltpu.make_async_copy(matrix_ref.at[:, 0, :], out_ref, sem)
    copy.start()
    copy.wait()


def product_kernel(place, own_ref, other_ref, a0_ref, a1_ref, high_ref, low_ref, terms_ref, gram_ref):
    start = pl.program_id(0) == 0

    @pl.when(start)
    def _():
        terms_ref[...] = jnp.zeros_like(terms_ref)
        gram_ref[...] = jnp.zeros_like(gram_ref)

    first = place[1] == 0
    own, other = own_ref[...], other_ref[...]
    panel = split(jnp.concatenate([jnp.where(first, own, other), jnp.where(first, other, own)], axis=1))
    high_ref[...], low_ref[...] = panel
    gram_ref[...] += three_pass(panel, panel, by_rows)
    for l in range(a0_ref.shape[1]):
        a = split(jnp.concatenate([a0_ref[:, l, :], a1_ref[:, l, :]], axis=0))
        part = three_pass(panel, a, by_rows)
        for r in range(PEERS):
            terms_ref[r, :SHARE, l * BLOCK : (l + 1) * BLOCK] += part[r * SHARE : (r + 1) * SHARE]

    @pl.when(pl.program_id(0) == pl.num_programs(0) - 1)
    def _():
        for n in range(HALF_ROWS // 8):
            (i, j), (p, q) = (half[n // 16] for half in HALF)
            top = n % 16 * 8
            here = gram_ref[i * TILE + top : i * TILE + top + 8, j * TILE : (j + 1) * TILE]
            there = gram_ref[p * TILE + top : p * TILE + top + 8, q * TILE : (q + 1) * TILE]
            lane = n % TILES * TILE
            terms_ref[n // TILES, SHARE:, lane : lane + TILE] = jnp.where(first, here, there)


def factor_kernel(place, own_ref, other_ref, high_ref, low_ref, m_ref, qh_ref, ql_ref, s_ref, t_ref):
    first = place[1] == 0
    s_ref[...] = jnp.zeros_like(s_ref)
    t_ref[...] = jnp.zeros_like(t_ref)
    for n in range(HALF_ROWS // 8):
        (i, j), (p, q) = (half[n // 16] for half in HALF)
        top = n % 16 * 8
        lane = n % TILES * TILE
        own = own_ref[n // TILES, :, lane : lane + TILE]
        other = other_ref[n // TILES, :, lane : lane + TILE]
        s_ref[j, i * TILE + top : i * TILE + top + 8, :] = jnp.where(first, own, other)
        s_ref[q, p * TILE + top : p * TILE + top + 8, :] = jnp.where(first, other, own)

    @pl.loop(0, NB)
    def _(j):
        d = pl.multiple_of(j * TILE, TILE)
        mj = invert_factor(s_ref[j, pl.ds(d, TILE), :])
        mrow = mm(mj, t_ref[j], plain)
        lanes = lax.broadcasted_iota(jnp.int32, (TILE, FULL), 1)
        mrow = jnp.where(lanes // TILE == j, jnp.concatenate([mj] * NB, axis=1), mrow)
        m_ref[pl.ds(d, TILE), :] = mrow
        rows = lax.broadcasted_iota(jnp.int32, (FULL, TILE), 0)
        low = jnp.where(rows >= d + TILE, mm(s_ref[j], mj, by_cols), 0.0)
        for i in range(1, NB):

            @pl.when(i > j)
            def _():
                part = low[i * TILE : (i + 1) * TILE]
                s_ref[i] -= mm(low, part, by_cols)
                t_ref[i] -= mm(part, mrow, plain)

    factor = split(m_ref[...])
    step = 2 * PIECE
    for g in range(0, DEPTH, 2):
        window = slice(g * PIECE, g * PIECE + step)
        q = split(three_pass((high_ref[window], low_ref[window]), factor, by_cols))
        for e in range(2):
            spot = pl.ds(pl.multiple_of(lax.rem(place[0] + g + e, DEPTH) * PIECE, PIECE), PIECE)
            qh_ref[spot, :] = q[0][e * PIECE : (e + 1) * PIECE]
            ql_ref[spot, :] = q[1][e * PIECE : (e + 1) * PIECE]


def remainder_kernel(place, qh_ref, ql_ref, a_ref, m_ref, w_ref, coeff_ref, out_ref, ch_ref, cl_ref):
    width = a_ref.shape[2]

    @pl.when(pl.program_id(0) == 0)
    def _():
        coeffs = three_pass(split(m_ref[...]), split(w_ref[...]), plain)
        for l in range(coeff_ref.shape[1]):
            coeff_ref[:, l, :] = coeffs[:, l * width : (l + 1) * width]
        ch_ref[...], cl_ref[...] = split(coeffs)

    q = qh_ref[...], ql_ref[...]
    for l in range(a_ref.shape[1]):
        window = slice(l * width, (l + 1) * width)
        out_ref[:, l, :] = a_ref[:, l, :] - three_pass(q, (ch_ref[:, window], cl_ref[:, window]), plain)


def call(kernel, name, mib, grid, ins, outs, out_shape, scratch=()):
    return pl.pallas_call(
        kernel,
        out_shape=out_shape,
        grid_spec=pltpu.PrefetchScalarGridSpec(
            num_scalar_prefetch=1, grid=grid, in_specs=ins, out_specs=outs, scratch_shapes=scratch
        ),
        compiler_params=pltpu.CompilerParams(vmem_limit_bytes=mib << 20),
        name=name,
    )


def whole(*shape):
    return pl.BlockSpec(shape, lambda g, place: (0,) * len(shape))


def f32(*shape):
    return jax.ShapeDtypeStruct(shape, jnp.float32)


def bf16(*shape):
    return pltpu.HBM(shape, jnp.bfloat16)


def in_hbm(*arrays):
    return [pltpu.with_memory_space_constraint(x, pltpu.HBM) for x in arrays]


def shift(x, axis, by):
    return lax.ppermute(x, axis, [(i, (i + by) % PEERS) for i in range(PEERS)])


def everywhere(share):
    return lax.all_to_all(jnp.broadcast_to(share, (PEERS,) + share.shape), "row", 0, 0)


def swap_cores(x):
    return lax.ppermute(x, "col", [(i, i ^ 1) for i in range(PEERS)])


def share_panel(mine, z):
    own = jnp.where(z == 0, mine[:PIECE], jnp.zeros((PIECE, BLOCK), jnp.float32))
    for k in range(1, DEPTH):
        own = own + lax.ppermute(mine[k * PIECE : (k + 1) * PIECE], "col", [(0, 2 * k), (1, 2 * k + 1)])
    up, down = [own], [own]
    for _ in range(DEPTH // 2 - 1):
        up.append(shift(up[-1], "col", 2))
        down.append(shift(down[-1], "col", -2))
    half = PIECE // 2
    far = [shift(up[-1][:half], "col", 2), shift(down[-1][half:], "col", -2)]
    return jnp.concatenate(down + far + up[:0:-1], axis=0)


def on_device(matrix):
    rows, blocks, width = matrix.shape
    col = lax.axis_index("col")
    z, core, row = col // 2, col % 2, lax.axis_index("row")
    place = jnp.stack([z, core, row]).astype(jnp.int32)

    mine = pl.pallas_call(
        panel_kernel,
        in_specs=[pl.BlockSpec(memory_space=pl.ANY)],
        out_specs=pl.BlockSpec(memory_space=pltpu.VMEM),
        out_shape=f32(rows, width),
        scratch_shapes=[pltpu.SemaphoreType.DMA],
        name="panel",
    )(matrix)
    own = share_panel(mine, z)
    other = swap_cores(own)

    step = 2 * PIECE
    steps = rows // step
    own_spec = pl.BlockSpec((step, BLOCK), lambda g, place: (g, 0))
    panel_spec = pl.BlockSpec((step, FULL), lambda g, place: (g, 0))
    high, low, terms = call(
        product_kernel, "product", 20, (steps,),
        [own_spec, own_spec]
        + [
            pl.BlockSpec((PIECE, blocks, width), lambda g, place, e=e: (lax.rem(place[0] + 2 * g + e, DEPTH), 0, 0))
            for e in range(2)
        ],
        [panel_spec, panel_spec, whole(PEERS, SHARE + 8, blocks * width)],
        [bf16(rows, FULL), bf16(rows, FULL), f32(PEERS, SHARE + 8, blocks * width)],
        [pltpu.VMEM((FULL, FULL), jnp.float32)],
    )(place, own, other, *in_hbm(matrix, matrix))
    total = jnp.sum(lax.all_to_all(terms, "row", 0, 0), axis=0)
    gram = everywhere(total[SHARE:, : TILES * TILE])
    sums = everywhere(total[:SHARE]).reshape(FULL, blocks * width)

    m, qh, ql = call(
        factor_kernel, "factor", 20, (1,),
        [whole(PEERS, 8, TILES * TILE)] * 2 + [whole(rows, FULL)] * 2,
        [whole(FULL, FULL), whole(rows, FULL), whole(rows, FULL)],
        [f32(FULL, FULL), bf16(rows, FULL), bf16(rows, FULL)],
        [pltpu.VMEM((NB, FULL, TILE), jnp.float32), pltpu.VMEM((NB, TILE, FULL), jnp.float32)],
    )(place, gram, swap_cores(gram), *in_hbm(high, low))

    a_spec = pl.BlockSpec((step, blocks, width), lambda g, place: (g, 0, 0))
    return call(
        remainder_kernel, "remainder", 22, (steps,),
        [panel_spec, panel_spec, a_spec, whole(FULL, FULL), whole(FULL, blocks * width)],
        [whole(FULL, blocks, width), a_spec],
        [f32(FULL, blocks, width), f32(rows, blocks, width)],
        [pltpu.VMEM((FULL, blocks * width), jnp.bfloat16)] * 2,
    )(place, *in_hbm(qh, ql, matrix), m, sums)


def solution(mesh):
    return jax.shard_map(
        on_device,
        mesh=mesh,
        in_specs=(P("row", None, "col"),),
        out_specs=(P(None, None, "col"), P("row", None, "col")),
        check_vma=False,
    )
```

```python
import jax
import jax.numpy as jnp
from jax import lax
from jax.experimental import pallas as pl
from jax.experimental.pallas import tpu as pltpu
from jax.sharding import PartitionSpec as P

BLOCK = 256
TILE = 128
NB = 4
STRIP = 8
FULL = NB * TILE
PEERS = 16
DEPTH = 8
PIECE = 128
HALF = ((0, 0), (1, 0), (1, 1), (2, 0), (2, 1)), ((2, 2), (3, 0), (3, 1), (3, 2), (3, 3))
HALF_ROWS = len(HALF[0]) * TILE
SHARE = FULL // PEERS
TILES = HALF_ROWS // 8 // PEERS

highest = lax.Precision.HIGHEST
by_rows = ((0,), (0,))
plain = ((1,), (0,))
by_cols = ((1,), (1,))


def mm(a, b, dims):
    return lax.dot_general(a, b, (dims, ((), ())), precision=highest, preferred_element_type=jnp.float32)

def invert_factor(s):
    n = TILE
    rows = lax.broadcasted_iota(jnp.int32, (n, n), 0)
    cols = lax.broadcasted_iota(jnp.int32, (n, n), 1)
    t = jnp.where(rows == cols, 1.0, 0.0).astype(jnp.float32)
    s_done, t_done = [], []
    for k in range(0, n, STRIP):
        top = (k // 8) * 8
        off = k - top
        height = n - top
        sub = lax.broadcasted_iota(jnp.int32, (height, n), 0)
        col = [jnp.broadcast_to(s[:, k + m : k + m + 1], (height, n)) for m in range(STRIP)]
        pivot = [[jnp.broadcast_to(col[j][off + i : off + i + 1, :], (8, n)) for j in range(STRIP)] for i in range(STRIP)]
        srow = [jnp.broadcast_to(s[off + m : off + m + 1, :], (8, n)) for m in range(STRIP)]
        trow = [jnp.broadcast_to(t[off + m : off + m + 1, :], (8, n)) for m in range(STRIP)]
        inv = []
        for m in range(STRIP):
            inv.append(1.0 / pivot[m][m])
            for i in range(m + 1, STRIP):
                low = pivot[i][m] * inv[m]
                for j in range(m + 1, STRIP):
                    if j <= i:
                        pivot[i][j] = pivot[i][j] - low * pivot[j][m]
                srow[i] = srow[i] - low * srow[m]
                trow[i] = trow[i] - low * trow[m]
        def tall(x):
            return jnp.concatenate([x] * (height // 8), axis=0) if height > 8 else x
        factor = []
        for m in range(STRIP):
            f = col[m]
            for j in range(m):
                f = f - factor[j] * tall(pivot[m][j])
            f = f * tall(inv[m])
            factor.append(f)
        for m in range(STRIP):
            f = jnp.where(sub > off + m, factor[m], 0.0)
            s = s - f * tall(srow[m])
            t = t - f * tall(trow[m])
        if off + STRIP == 8:
            s_done.append(s[:8])
            t_done.append(t[:8])
            if height > 8:
                s, t = s[8:], t[8:]
    s = jnp.concatenate(s_done, axis=0)
    t = jnp.concatenate(t_done, axis=0)
    diag = jnp.sum(jnp.where(rows == cols, s, 0.0), axis=1, keepdims=True)
    return t * lax.rsqrt(diag)


def split(x):
    high = x.astype(jnp.bfloat16)
    return high, (x - high.astype(jnp.float32)).astype(jnp.bfloat16)


def one_pass(a, b, dims):
    return lax.dot_general(a, b, (dims, ((), ())), preferred_element_type=jnp.float32)


def three_pass(a, b, dims):
    return one_pass(a[0], b[0], dims) + (one_pass(a[0], b[1], dims) + one_pass(a[1], b[0], dims))


def panel_kernel(matrix_ref, *refs):
    outs, sems = refs[:-1], refs[-1]
    copies = [
        pltpu.make_async_copy(matrix_ref.at[k * PIECE : (k + 1) * PIECE, 0, :], out, sems.at[k]) for k, out in enumerate(outs)
    ]
    for copy in copies:
        copy.start()
    for copy in copies:
        copy.wait()


def product_kernel(place, own_ref, other_ref, a_ref, high_ref, low_ref, terms_ref, gram_ref):
    start = pl.program_id(0) == 0

    @pl.when(start)
    def _():
        terms_ref[...] = jnp.zeros_like(terms_ref)
        gram_ref[...] = jnp.zeros_like(gram_ref)

    first = place[1] == 0
    own, other = own_ref[...], other_ref[...]
    panel = split(jnp.concatenate([jnp.where(first, own, other), jnp.where(first, other, own)], axis=1))
    high_ref[...], low_ref[...] = panel
    gram_ref[...] += three_pass(panel, panel, by_rows)
    for l in range(a_ref.shape[1]):
        a = split(a_ref[:, l, :])
        part = three_pass(panel, a, by_rows)
        for r in range(PEERS):
            terms_ref[r, :SHARE, l * BLOCK : (l + 1) * BLOCK] += part[r * SHARE : (r + 1) * SHARE]

    @pl.when(pl.program_id(0) == pl.num_programs(0) - 1)
    def _():
        for n in range(HALF_ROWS // 8):
            (i, j), (p, q) = (half[n // 16] for half in HALF)
            top = n % 16 * 8
            here = gram_ref[i * TILE + top : i * TILE + top + 8, j * TILE : (j + 1) * TILE]
            there = gram_ref[p * TILE + top : p * TILE + top + 8, q * TILE : (q + 1) * TILE]
            lane = n % TILES * TILE
            terms_ref[n // TILES, SHARE:, lane : lane + TILE] = jnp.where(first, here, there)


def factor_kernel(place, own_ref, other_ref, high_ref, low_ref, m_ref, qh_ref, ql_ref, s_ref, t_ref):
    first = place[1] == 0
    s_ref[...] = jnp.zeros_like(s_ref)
    t_ref[...] = jnp.zeros_like(t_ref)
    for n in range(HALF_ROWS // 8):
        (i, j), (p, q) = (half[n // 16] for half in HALF)
        top = n % 16 * 8
        lane = n % TILES * TILE
        own = own_ref[n // TILES, :, lane : lane + TILE]
        other = other_ref[n // TILES, :, lane : lane + TILE]
        s_ref[j, i * TILE + top : i * TILE + top + 8, :] = jnp.where(first, own, other)
        s_ref[q, p * TILE + top : p * TILE + top + 8, :] = jnp.where(first, other, own)

    def update(j, i, k):
        s_ref[k, i * TILE : (i + 1) * TILE, :] -= mm(low[i], low[k], by_cols)

    for j in range(NB):
        d = j * TILE
        mj = invert_factor(s_ref[j, d : d + TILE, :])
        if j:
            done = j - 1
            for i in range(j, NB):
                t_ref[i, :, :d] -= mm(low[i], m_ref[done * TILE : d, :d], plain)
                for k in range(j, i + 1):
                    if i > j:
                        update(done, i, k)
            m_ref[d : d + TILE, :d] = mm(mj, t_ref[j, :, :d], plain)
        m_ref[d : d + TILE, d : d + TILE] = mj
        if j + 1 < NB:
            m_ref[d : d + TILE, d + TILE :] = jnp.zeros((TILE, FULL - d - TILE), jnp.float32)
            column = mm(s_ref[j, d + TILE :, :], mj, by_cols)
            low = {i: column[(i - j - 1) * TILE : (i - j) * TILE] for i in range(j + 1, NB)}
            update(j, j + 1, j + 1)

    factor = split(m_ref[...])
    step = 2 * PIECE
    for g in range(0, qh_ref.shape[0], step):
        window = slice(g, g + step)
        qh_ref[window], ql_ref[window] = split(three_pass((high_ref[window], low_ref[window]), factor, by_cols))


def remainder_kernel(place, qh_ref, ql_ref, a_ref, m_ref, w_ref, coeff_ref, out_ref, ch_ref, cl_ref):
    width = a_ref.shape[2]

    @pl.when(pl.program_id(0) == 0)
    def _():
        coeffs = three_pass(split(m_ref[...]), split(w_ref[...]), plain)
        for l in range(coeff_ref.shape[1]):
            coeff_ref[:, l, :] = coeffs[:, l * width : (l + 1) * width]
        ch_ref[...], cl_ref[...] = split(coeffs)

    q = qh_ref[...], ql_ref[...]
    for l in range(a_ref.shape[1]):
        window = slice(l * width, (l + 1) * width)
        out_ref[:, l, :] = a_ref[:, l, :] - three_pass(q, (ch_ref[:, window], cl_ref[:, window]), plain)


def call(kernel, name, mib, grid, ins, outs, out_shape, scratch=()):
    return pl.pallas_call(
        kernel,
        out_shape=out_shape,
        grid_spec=pltpu.PrefetchScalarGridSpec(
            num_scalar_prefetch=1, grid=grid, in_specs=ins, out_specs=outs, scratch_shapes=scratch
        ),
        compiler_params=pltpu.CompilerParams(vmem_limit_bytes=mib << 20),
        name=name,
    )


def whole(*shape):
    return pl.BlockSpec(shape, lambda g, place: (0,) * len(shape))


def f32(*shape):
    return jax.ShapeDtypeStruct(shape, jnp.float32)


def bf16(*shape):
    return pltpu.HBM(shape, jnp.bfloat16)


def in_hbm(*arrays):
    return [pltpu.with_memory_space_constraint(x, pltpu.HBM) for x in arrays]


def everywhere(share):
    return lax.all_to_all(jnp.broadcast_to(share, (PEERS,) + share.shape), "row", 0, 0)


def swap_cores(x):
    return lax.ppermute(x, "col", [(i, i ^ 1) for i in range(PEERS)])


def share_panel(mine, z):
    own = jnp.where(z == 0, mine[0], jnp.zeros((PIECE, BLOCK), jnp.float32))
    for k in range(1, DEPTH):
        own = own + lax.ppermute(mine[k], "col", [(0, 2 * k), (1, 2 * k + 1)])
    groups = [[2 * k + core for k in range(DEPTH)] for core in range(2)]
    pieces = lax.all_to_all(jnp.broadcast_to(own, (DEPTH,) + own.shape), "col", 0, 0, axis_index_groups=groups)
    return pieces.reshape(DEPTH * PIECE, BLOCK)


def on_device(matrix):
    rows, blocks, width = matrix.shape
    col = lax.axis_index("col")
    z, core, row = col // 2, col % 2, lax.axis_index("row")
    place = jnp.stack([z, core, row]).astype(jnp.int32)

    mine = pl.pallas_call(
        panel_kernel,
        in_specs=[pl.BlockSpec(memory_space=pl.ANY)],
        out_specs=[pl.BlockSpec(memory_space=pltpu.VMEM)] * DEPTH,
        out_shape=[f32(PIECE, width)] * DEPTH,
        scratch_shapes=[pltpu.SemaphoreType.DMA((DEPTH,))],
        name="panel",
    )(*in_hbm(matrix))
    own = share_panel(mine, z)
    other = swap_cores(own)

    step = 2 * PIECE
    steps = rows // step
    own_spec = pl.BlockSpec((step, BLOCK), lambda g, place: (g, 0))
    panel_spec = pl.BlockSpec((step, FULL), lambda g, place: (g, 0))
    a_spec = pl.BlockSpec((step, blocks, width), lambda g, place: (g, 0, 0))
    high, low, terms = call(
        product_kernel, "product", 20, (steps,),
        [own_spec, own_spec, a_spec],
        [panel_spec, panel_spec, whole(PEERS, SHARE + 8, blocks * width)],
        [bf16(rows, FULL), bf16(rows, FULL), f32(PEERS, SHARE + 8, blocks * width)],
        [pltpu.VMEM((FULL, FULL), jnp.float32)],
    )(place, own, other, *in_hbm(matrix))
    total = jnp.sum(lax.all_to_all(terms, "row", 0, 0), axis=0)
    sums = lax.all_gather(total[:SHARE], "row", tiled=True)
    gram = everywhere(total[SHARE:, : TILES * TILE])

    m, qh, ql = call(
        factor_kernel, "factor", 20, (1,),
        [whole(PEERS, 8, TILES * TILE)] * 2 + [whole(rows, FULL)] * 2,
        [whole(FULL, FULL), whole(rows, FULL), whole(rows, FULL)],
        [f32(FULL, FULL), bf16(rows, FULL), bf16(rows, FULL)],
        [pltpu.VMEM((NB, FULL, TILE), jnp.float32), pltpu.VMEM((NB, TILE, FULL), jnp.float32)],
    )(place, gram, swap_cores(gram), *in_hbm(high, low))

    return call(
        remainder_kernel, "remainder", 22, (steps,),
        [panel_spec, panel_spec, a_spec, whole(FULL, FULL), whole(FULL, blocks * width)],
        [whole(FULL, blocks, width), a_spec],
        [f32(FULL, blocks, width), f32(rows, blocks, width)],
        [pltpu.VMEM((FULL, blocks * width), jnp.bfloat16)] * 2,
    )(place, *in_hbm(qh, ql, matrix), m, sums)


def solution(mesh):
    return jax.shard_map(
        on_device,
        mesh=mesh,
        in_specs=(P("row", None, "col"),),
        out_specs=(P(None, None, "col"), P("row", None, "col")),
        check_vma=False,
    )
```

```python
import jax
import jax.numpy as jnp
from jax import lax
from jax.experimental import pallas as pl
from jax.experimental.pallas import tpu as pltpu
from jax.sharding import PartitionSpec as P

BLOCK = 256
TILE = 128
NB = 4
STRIP = 8
FULL = NB * TILE
PEERS = 16
DEPTH = 8
PIECE = 128
HALF = ((0, 0), (1, 0), (1, 1), (2, 0), (2, 1)), ((2, 2), (3, 0), (3, 1), (3, 2), (3, 3))
HALF_ROWS = len(HALF[0]) * TILE
SHARE = FULL // PEERS
TILES = HALF_ROWS // 8 // PEERS

highest = lax.Precision.HIGHEST
by_rows = ((0,), (0,))
plain = ((1,), (0,))
by_cols = ((1,), (1,))


def mm(a, b, dims):
    return lax.dot_general(a, b, (dims, ((), ())), precision=highest, preferred_element_type=jnp.float32)

def invert_factor(s):
    n = TILE
    rows = lax.broadcasted_iota(jnp.int32, (n, n), 0)
    cols = lax.broadcasted_iota(jnp.int32, (n, n), 1)
    t = jnp.where(rows == cols, 1.0, 0.0).astype(jnp.float32)
    s_done, t_done = [], []
    for k in range(0, n, STRIP):
        top = (k // 8) * 8
        off = k - top
        height = n - top
        sub = lax.broadcasted_iota(jnp.int32, (height, n), 0)
        col = [jnp.broadcast_to(s[:, k + m : k + m + 1], (height, n)) for m in range(STRIP)]
        pivot = [[jnp.broadcast_to(col[j][off + i : off + i + 1, :], (8, n)) for j in range(STRIP)] for i in range(STRIP)]
        srow = [jnp.broadcast_to(s[off + m : off + m + 1, :], (8, n)) for m in range(STRIP)]
        trow = [jnp.broadcast_to(t[off + m : off + m + 1, :], (8, n)) for m in range(STRIP)]
        inv = []
        for m in range(STRIP):
            inv.append(1.0 / pivot[m][m])
            for i in range(m + 1, STRIP):
                low = pivot[i][m] * inv[m]
                for j in range(m + 1, STRIP):
                    if j <= i:
                        pivot[i][j] = pivot[i][j] - low * pivot[j][m]
                srow[i] = srow[i] - low * srow[m]
                trow[i] = trow[i] - low * trow[m]
        def tall(x):
            return jnp.concatenate([x] * (height // 8), axis=0) if height > 8 else x
        factor = []
        for m in range(STRIP):
            f = col[m]
            for j in range(m):
                f = f - factor[j] * tall(pivot[m][j])
            f = f * tall(inv[m])
            factor.append(f)
        for m in range(STRIP):
            f = jnp.where(sub > off + m, factor[m], 0.0)
            s = s - f * tall(srow[m])
            t = t - f * tall(trow[m])
        if off + STRIP == 8:
            s_done.append(s[:8])
            t_done.append(t[:8])
            if height > 8:
                s, t = s[8:], t[8:]
    s = jnp.concatenate(s_done, axis=0)
    t = jnp.concatenate(t_done, axis=0)
    diag = jnp.sum(jnp.where(rows == cols, s, 0.0), axis=1, keepdims=True)
    return t * lax.rsqrt(diag)


def split(x):
    high = x.astype(jnp.bfloat16)
    return high, (x - high.astype(jnp.float32)).astype(jnp.bfloat16)


def one_pass(a, b, dims):
    return lax.dot_general(a, b, (dims, ((), ())), preferred_element_type=jnp.float32)


def three_pass(a, b, dims):
    return one_pass(a[0], b[0], dims) + (one_pass(a[0], b[1], dims) + one_pass(a[1], b[0], dims))


def panel_kernel(matrix_ref, *refs):
    outs, sems = refs[:-1], refs[-1]
    copies = [
        pltpu.make_async_copy(matrix_ref.at[k * PIECE : (k + 1) * PIECE, 0, :], out, sems.at[k]) for k, out in enumerate(outs)
    ]
    for copy in copies:
        copy.start()
    for copy in copies:
        copy.wait()


def product_kernel(place, own_ref, other_ref, a0_ref, a1_ref, high_ref, low_ref, terms_ref, gram_ref):
    start = pl.program_id(0) == 0

    @pl.when(start)
    def _():
        terms_ref[...] = jnp.zeros_like(terms_ref)
        gram_ref[...] = jnp.zeros_like(gram_ref)

    first = place[1] == 0
    own, other = own_ref[...], other_ref[...]
    panel = split(jnp.concatenate([jnp.where(first, own, other), jnp.where(first, other, own)], axis=1))
    high_ref[...], low_ref[...] = panel
    gram_ref[...] += three_pass(panel, panel, by_rows)
    for l in range(a0_ref.shape[1]):
        a = split(jnp.concatenate([a0_ref[:, l, :], a1_ref[:, l, :]], axis=0))
        part = three_pass(panel, a, by_rows)
        for r in range(PEERS):
            terms_ref[r, :SHARE, l * BLOCK : (l + 1) * BLOCK] += part[r * SHARE : (r + 1) * SHARE]

    @pl.when(pl.program_id(0) == pl.num_programs(0) - 1)
    def _():
        for n in range(HALF_ROWS // 8):
            (i, j), (p, q) = (half[n // 16] for half in HALF)
            top = n % 16 * 8
            here = gram_ref[i * TILE + top : i * TILE + top + 8, j * TILE : (j + 1) * TILE]
            there = gram_ref[p * TILE + top : p * TILE + top + 8, q * TILE : (q + 1) * TILE]
            lane = n % TILES * TILE
            terms_ref[n // TILES, SHARE:, lane : lane + TILE] = jnp.where(first, here, there)


def factor_kernel(place, own_ref, other_ref, high_ref, low_ref, m_ref, qh_ref, ql_ref, s_ref, t_ref):
    first = place[1] == 0
    s_ref[...] = jnp.zeros_like(s_ref)
    t_ref[...] = jnp.zeros_like(t_ref)
    for n in range(HALF_ROWS // 8):
        (i, j), (p, q) = (half[n // 16] for half in HALF)
        top = n % 16 * 8
        lane = n % TILES * TILE
        own = own_ref[n // TILES, :, lane : lane + TILE]
        other = other_ref[n // TILES, :, lane : lane + TILE]
        s_ref[j, i * TILE + top : i * TILE + top + 8, :] = jnp.where(first, own, other)
        s_ref[q, p * TILE + top : p * TILE + top + 8, :] = jnp.where(first, other, own)

    def update(j, i, k):
        s_ref[k, i * TILE : (i + 1) * TILE, :] -= mm(low[i], low[k], by_cols)

    for j in range(NB):
        d = j * TILE
        mj = invert_factor(s_ref[j, d : d + TILE, :])
        if j:
            done = j - 1
            for i in range(j, NB):
                t_ref[i, :, :d] -= mm(low[i], m_ref[done * TILE : d, :d], plain)
                for k in range(j, i + 1):
                    if i > j:
                        update(done, i, k)
            m_ref[d : d + TILE, :d] = mm(mj, t_ref[j, :, :d], plain)
        m_ref[d : d + TILE, d : d + TILE] = mj
        if j + 1 < NB:
            m_ref[d : d + TILE, d + TILE :] = jnp.zeros((TILE, FULL - d - TILE), jnp.float32)
            column = mm(s_ref[j, d + TILE :, :], mj, by_cols)
            low = {i: column[(i - j - 1) * TILE : (i - j) * TILE] for i in range(j + 1, NB)}
            update(j, j + 1, j + 1)

    factor = split(m_ref[...])
    step = 2 * PIECE
    for g in range(0, DEPTH, 2):
        window = slice(g * PIECE, g * PIECE + step)
        q = split(three_pass((high_ref[window], low_ref[window]), factor, by_cols))
        for e in range(2):
            spot = pl.ds(pl.multiple_of(lax.rem(place[0] + g + e, DEPTH) * PIECE, PIECE), PIECE)
            qh_ref[spot, :] = q[0][e * PIECE : (e + 1) * PIECE]
            ql_ref[spot, :] = q[1][e * PIECE : (e + 1) * PIECE]


def remainder_kernel(place, qh_ref, ql_ref, a_ref, m_ref, w_ref, coeff_ref, out_ref, ch_ref, cl_ref):
    width = a_ref.shape[2]

    @pl.when(pl.program_id(0) == 0)
    def _():
        coeffs = three_pass(split(m_ref[...]), split(w_ref[...]), plain)
        for l in range(coeff_ref.shape[1]):
            coeff_ref[:, l, :] = coeffs[:, l * width : (l + 1) * width]
        ch_ref[...], cl_ref[...] = split(coeffs)

    q = qh_ref[...], ql_ref[...]
    for l in range(a_ref.shape[1]):
        window = slice(l * width, (l + 1) * width)
        out_ref[:, l, :] = a_ref[:, l, :] - three_pass(q, (ch_ref[:, window], cl_ref[:, window]), plain)


def call(kernel, name, mib, grid, ins, outs, out_shape, scratch=()):
    return pl.pallas_call(
        kernel,
        out_shape=out_shape,
        grid_spec=pltpu.PrefetchScalarGridSpec(
            num_scalar_prefetch=1, grid=grid, in_specs=ins, out_specs=outs, scratch_shapes=scratch
        ),
        compiler_params=pltpu.CompilerParams(vmem_limit_bytes=mib << 20),
        name=name,
    )


def whole(*shape):
    return pl.BlockSpec(shape, lambda g, place: (0,) * len(shape))


def f32(*shape):
    return jax.ShapeDtypeStruct(shape, jnp.float32)


def bf16(*shape):
    return pltpu.HBM(shape, jnp.bfloat16)


def in_hbm(*arrays):
    return [pltpu.with_memory_space_constraint(x, pltpu.HBM) for x in arrays]


def shift(x, axis, by):
    return lax.ppermute(x, axis, [(i, (i + by) % PEERS) for i in range(PEERS)])


def everywhere(share):
    return lax.all_to_all(jnp.broadcast_to(share, (PEERS,) + share.shape), "row", 0, 0)


def swap_cores(x):
    return lax.ppermute(x, "col", [(i, i ^ 1) for i in range(PEERS)])


def share_panel(mine, z):
    own = jnp.where(z == 0, mine[0], jnp.zeros((PIECE, BLOCK), jnp.float32))
    for k in range(1, DEPTH):
        own = own + lax.ppermute(mine[k], "col", [(0, 2 * k), (1, 2 * k + 1)])
    up, down = [own], [own]
    for _ in range(DEPTH // 2 - 1):
        up.append(shift(up[-1], "col", 2))
        down.append(shift(down[-1], "col", -2))
    half = PIECE // 2
    far = [shift(up[-1][:half], "col", 2), shift(down[-1][half:], "col", -2)]
    return jnp.concatenate(down + far + up[:0:-1], axis=0)


def on_device(matrix):
    rows, blocks, width = matrix.shape
    col = lax.axis_index("col")
    z, core, row = col // 2, col % 2, lax.axis_index("row")
    place = jnp.stack([z, core, row]).astype(jnp.int32)

    mine = pl.pallas_call(
        panel_kernel,
        in_specs=[pl.BlockSpec(memory_space=pl.ANY)],
        out_specs=[pl.BlockSpec(memory_space=pltpu.VMEM)] * DEPTH,
        out_shape=[f32(PIECE, width)] * DEPTH,
        scratch_shapes=[pltpu.SemaphoreType.DMA((DEPTH,))],
        name="panel",
    )(*in_hbm(matrix))
    own = share_panel(mine, z)
    other = swap_cores(own)

    step = 2 * PIECE
    steps = rows // step
    own_spec = pl.BlockSpec((step, BLOCK), lambda g, place: (g, 0))
    panel_spec = pl.BlockSpec((step, FULL), lambda g, place: (g, 0))
    high, low, terms = call(
        product_kernel, "product", 20, (steps,),
        [own_spec, own_spec]
        + [
            pl.BlockSpec((PIECE, blocks, width), lambda g, place, e=e: (lax.rem(place[0] + 2 * g + e, DEPTH), 0, 0))
            for e in range(2)
        ],
        [panel_spec, panel_spec, whole(PEERS, SHARE + 8, blocks * width)],
        [bf16(rows, FULL), bf16(rows, FULL), f32(PEERS, SHARE + 8, blocks * width)],
        [pltpu.VMEM((FULL, FULL), jnp.float32)],
    )(place, own, other, *in_hbm(matrix, matrix))
    total = jnp.sum(lax.all_to_all(terms, "row", 0, 0), axis=0)
    gram = everywhere(total[SHARE:, : TILES * TILE])
    sums = everywhere(total[:SHARE]).reshape(FULL, blocks * width)

    m, qh, ql = call(
        factor_kernel, "factor", 20, (1,),
        [whole(PEERS, 8, TILES * TILE)] * 2 + [whole(rows, FULL)] * 2,
        [whole(FULL, FULL), whole(rows, FULL), whole(rows, FULL)],
        [f32(FULL, FULL), bf16(rows, FULL), bf16(rows, FULL)],
        [pltpu.VMEM((NB, FULL, TILE), jnp.float32), pltpu.VMEM((NB, TILE, FULL), jnp.float32)],
    )(place, gram, swap_cores(gram), *in_hbm(high, low))

    a_spec = pl.BlockSpec((step, blocks, width), lambda g, place: (g, 0, 0))
    return call(
        remainder_kernel, "remainder", 22, (steps,),
        [panel_spec, panel_spec, a_spec, whole(FULL, FULL), whole(FULL, blocks * width)],
        [whole(FULL, blocks, width), a_spec],
        [f32(FULL, blocks, width), f32(rows, blocks, width)],
        [pltpu.VMEM((FULL, blocks * width), jnp.bfloat16)] * 2,
    )(place, *in_hbm(qh, ql, matrix), m, sums)


def solution(mesh):
    return jax.shard_map(
        on_device,
        mesh=mesh,
        in_specs=(P("row", None, "col"),),
        out_specs=(P(None, None, "col"), P("row", None, "col")),
        check_vma=False,
    )
```

```python
import jax
import jax.numpy as jnp
from jax import lax
from jax.experimental import pallas as pl
from jax.experimental.pallas import tpu as pltpu
from jax.sharding import PartitionSpec as P

BLOCK = 256
TILE = 128
NB = 4
STRIP = 8
FULL = NB * TILE
PEERS = 16
DEPTH = 8
PIECE = 128
HALF = ((0, 0), (1, 0), (1, 1), (2, 0), (2, 1)), ((2, 2), (3, 0), (3, 1), (3, 2), (3, 3))
HALF_ROWS = len(HALF[0]) * TILE
SHARE = FULL // PEERS
TILES = HALF_ROWS // 8 // PEERS

highest = lax.Precision.HIGHEST
by_rows = ((0,), (0,))
plain = ((1,), (0,))
by_cols = ((1,), (1,))


def mm(a, b, dims):
    return lax.dot_general(a, b, (dims, ((), ())), precision=highest, preferred_element_type=jnp.float32)

def invert_factor(s):
    n = TILE
    rows = lax.broadcasted_iota(jnp.int32, (n, n), 0)
    cols = lax.broadcasted_iota(jnp.int32, (n, n), 1)
    t = jnp.where(rows == cols, 1.0, 0.0).astype(jnp.float32)
    s_done, t_done = [], []
    for k in range(0, n, STRIP):
        top = (k // 8) * 8
        off = k - top
        height = n - top
        sub = lax.broadcasted_iota(jnp.int32, (height, n), 0)
        col = [jnp.broadcast_to(s[:, k + m : k + m + 1], (height, n)) for m in range(STRIP)]
        pivot = [[jnp.broadcast_to(col[j][off + i : off + i + 1, :], (8, n)) for j in range(STRIP)] for i in range(STRIP)]
        srow = [jnp.broadcast_to(s[off + m : off + m + 1, :], (8, n)) for m in range(STRIP)]
        trow = [jnp.broadcast_to(t[off + m : off + m + 1, :], (8, n)) for m in range(STRIP)]
        inv = []
        for m in range(STRIP):
            inv.append(1.0 / pivot[m][m])
            for i in range(m + 1, STRIP):
                low = pivot[i][m] * inv[m]
                for j in range(m + 1, STRIP):
                    if j <= i:
                        pivot[i][j] = pivot[i][j] - low * pivot[j][m]
                srow[i] = srow[i] - low * srow[m]
                trow[i] = trow[i] - low * trow[m]
        def tall(x):
            return jnp.concatenate([x] * (height // 8), axis=0) if height > 8 else x
        factor = []
        for m in range(STRIP):
            f = col[m]
            for j in range(m):
                f = f - factor[j] * tall(pivot[m][j])
            f = f * tall(inv[m])
            factor.append(f)
        for m in range(STRIP):
            f = jnp.where(sub > off + m, factor[m], 0.0)
            s = s - f * tall(srow[m])
            t = t - f * tall(trow[m])
        if off + STRIP == 8:
            s_done.append(s[:8])
            t_done.append(t[:8])
            if height > 8:
                s, t = s[8:], t[8:]
    s = jnp.concatenate(s_done, axis=0)
    t = jnp.concatenate(t_done, axis=0)
    diag = jnp.sum(jnp.where(rows == cols, s, 0.0), axis=1, keepdims=True)
    return t * lax.rsqrt(diag)


def split(x):
    high = x.astype(jnp.bfloat16)
    return high, (x - high.astype(jnp.float32)).astype(jnp.bfloat16)


def one_pass(a, b, dims):
    return lax.dot_general(a, b, (dims, ((), ())), preferred_element_type=jnp.float32)


def three_pass(a, b, dims):
    return one_pass(a[0], b[0], dims) + (one_pass(a[0], b[1], dims) + one_pass(a[1], b[0], dims))


def panel_kernel(matrix_ref, *refs):
    outs, sems = refs[:-1], refs[-1]
    copies = [
        pltpu.make_async_copy(matrix_ref.at[k * PIECE : (k + 1) * PIECE, 0, :], out, sems.at[k]) for k, out in enumerate(outs)
    ]
    for copy in copies:
        copy.start()
    for copy in copies:
        copy.wait()


def product_kernel(place, own_ref, other_ref, a0_ref, a1_ref, high_ref, low_ref, terms_ref, gram_ref):
    start = pl.program_id(0) == 0

    @pl.when(start)
    def _():
        terms_ref[...] = jnp.zeros_like(terms_ref)
        gram_ref[...] = jnp.zeros_like(gram_ref)

    first = place[1] == 0
    own, other = own_ref[...], other_ref[...]
    panel = split(jnp.concatenate([jnp.where(first, own, other), jnp.where(first, other, own)], axis=1))
    high_ref[...], low_ref[...] = panel
    gram_ref[...] += three_pass(panel, panel, by_rows)
    for l in range(a0_ref.shape[1]):
        a = split(jnp.concatenate([a0_ref[:, l, :], a1_ref[:, l, :]], axis=0))
        part = three_pass(panel, a, by_rows)
        for r in range(PEERS):
            for e in range(BLOCK // TILE):
                spot = slice((l * BLOCK // TILE + e) * SHARE, (l * BLOCK // TILE + e + 1) * SHARE)
                terms_ref[r, spot, :] += part[r * SHARE : (r + 1) * SHARE, e * TILE : (e + 1) * TILE]

    @pl.when(pl.program_id(0) == pl.num_programs(0) - 1)
    def _():
        for n in range(HALF_ROWS // 8):
            (i, j), (p, q) = (half[n // 16] for half in HALF)
            top = n % 16 * 8
            here = gram_ref[i * TILE + top : i * TILE + top + 8, j * TILE : (j + 1) * TILE]
            there = gram_ref[p * TILE + top : p * TILE + top + 8, q * TILE : (q + 1) * TILE]
            spot = terms_ref.shape[1] + (n % TILES - TILES) * 8
            terms_ref[n // TILES, spot : spot + 8, :] = jnp.where(first, here, there)


def factor_kernel(place, own_ref, other_ref, high_ref, low_ref, m_ref, qh_ref, ql_ref, s_ref, t_ref):
    first = place[1] == 0
    s_ref[...] = jnp.zeros_like(s_ref)
    t_ref[...] = jnp.zeros_like(t_ref)
    for n in range(HALF_ROWS // 8):
        (i, j), (p, q) = (half[n // 16] for half in HALF)
        top = n % 16 * 8
        spot = slice(n % TILES * 8, n % TILES * 8 + 8)
        own = own_ref[n // TILES, spot, :]
        other = other_ref[n // TILES, spot, :]
        s_ref[j, i * TILE + top : i * TILE + top + 8, :] = jnp.where(first, own, other)
        s_ref[q, p * TILE + top : p * TILE + top + 8, :] = jnp.where(first, other, own)

    def update(j, i, k):
        s_ref[k, i * TILE : (i + 1) * TILE, :] -= mm(low[i], low[k], by_cols)

    for j in range(NB):
        d = j * TILE
        mj = invert_factor(s_ref[j, d : d + TILE, :])
        if j:
            done = j - 1
            for i in range(j, NB):
                t_ref[i, :, :d] -= mm(low[i], m_ref[done * TILE : d, :d], plain)
                for k in range(j, i + 1):
                    if i > j:
                        update(done, i, k)
            m_ref[d : d + TILE, :d] = mm(mj, t_ref[j, :, :d], plain)
        m_ref[d : d + TILE, d : d + TILE] = mj
        if j + 1 < NB:
            m_ref[d : d + TILE, d + TILE :] = jnp.zeros((TILE, FULL - d - TILE), jnp.float32)
            column = mm(s_ref[j, d + TILE :, :], mj, by_cols)
            low = {i: column[(i - j - 1) * TILE : (i - j) * TILE] for i in range(j + 1, NB)}
            update(j, j + 1, j + 1)

    factor = split(m_ref[...])
    step = 2 * PIECE
    for g in range(0, DEPTH, 2):
        window = slice(g * PIECE, g * PIECE + step)
        q = split(three_pass((high_ref[window], low_ref[window]), factor, by_cols))
        for e in range(2):
            spot = pl.ds(pl.multiple_of(lax.rem(place[0] + g + e, DEPTH) * PIECE, PIECE), PIECE)
            qh_ref[spot, :] = q[0][e * PIECE : (e + 1) * PIECE]
            ql_ref[spot, :] = q[1][e * PIECE : (e + 1) * PIECE]


def remainder_kernel(place, qh_ref, ql_ref, a_ref, m_ref, w_ref, coeff_ref, out_ref, ch_ref, cl_ref):
    width = a_ref.shape[2]
    each = width // TILE

    @pl.when(pl.program_id(0) == 0)
    def _():
        factor = split(m_ref[...])
        for l in range(coeff_ref.shape[1]):
            tiles = [w_ref[:, t * SHARE : (t + 1) * SHARE, :].reshape(FULL, TILE) for t in range(l * each, (l + 1) * each)]
            coeffs = three_pass(factor, split(jnp.concatenate(tiles, axis=1)), plain)
            coeff_ref[:, l, :] = coeffs
            window = slice(l * width, (l + 1) * width)
            ch_ref[:, window], cl_ref[:, window] = split(coeffs)

    q = qh_ref[...], ql_ref[...]
    for l in range(a_ref.shape[1]):
        window = slice(l * width, (l + 1) * width)
        out_ref[:, l, :] = a_ref[:, l, :] - three_pass(q, (ch_ref[:, window], cl_ref[:, window]), plain)


def call(kernel, name, mib, grid, ins, outs, out_shape, scratch=()):
    return pl.pallas_call(
        kernel,
        out_shape=out_shape,
        grid_spec=pltpu.PrefetchScalarGridSpec(
            num_scalar_prefetch=1, grid=grid, in_specs=ins, out_specs=outs, scratch_shapes=scratch
        ),
        compiler_params=pltpu.CompilerParams(vmem_limit_bytes=mib << 20),
        name=name,
    )


def whole(*shape):
    return pl.BlockSpec(shape, lambda g, place: (0,) * len(shape))


def f32(*shape):
    return jax.ShapeDtypeStruct(shape, jnp.float32)


def bf16(*shape):
    return pltpu.HBM(shape, jnp.bfloat16)


def in_hbm(*arrays):
    return [pltpu.with_memory_space_constraint(x, pltpu.HBM) for x in arrays]


def shift(x, axis, by):
    return lax.ppermute(x, axis, [(i, (i + by) % PEERS) for i in range(PEERS)])


def everywhere(share):
    return lax.all_to_all(jnp.broadcast_to(share, (PEERS,) + share.shape), "row", 0, 0)


def swap_cores(x):
    return lax.ppermute(x, "col", [(i, i ^ 1) for i in range(PEERS)])


def share_panel(mine, z):
    own = jnp.where(z == 0, mine[0], jnp.zeros((PIECE, BLOCK), jnp.float32))
    for k in (3, 5, 4, 2, 6, 1, 7):
        own = own + lax.ppermute(mine[k], "col", [(0, 2 * k), (1, 2 * k + 1)])
    up, down = [own], [own]
    for _ in range(DEPTH // 2 - 1):
        up.append(shift(up[-1], "col", 2))
        down.append(shift(down[-1], "col", -2))
    half = PIECE // 2
    far = [shift(up[-1][:half], "col", 2), shift(down[-1][half:], "col", -2)]
    return jnp.concatenate(down + far + up[:0:-1], axis=0)


def on_device(matrix):
    rows, blocks, width = matrix.shape
    col = lax.axis_index("col")
    z, core, row = col // 2, col % 2, lax.axis_index("row")
    place = jnp.stack([z, core, row]).astype(jnp.int32)

    mine = pl.pallas_call(
        panel_kernel,
        in_specs=[pl.BlockSpec(memory_space=pl.ANY)],
        out_specs=[pl.BlockSpec(memory_space=pltpu.VMEM)] * DEPTH,
        out_shape=[f32(PIECE, width)] * DEPTH,
        scratch_shapes=[pltpu.SemaphoreType.DMA((DEPTH,))],
        name="panel",
    )(*in_hbm(matrix))
    own = share_panel(mine, z)
    other = swap_cores(own)

    step = 2 * PIECE
    steps = rows // step
    own_spec = pl.BlockSpec((step, BLOCK), lambda g, place: (g, 0))
    panel_spec = pl.BlockSpec((step, FULL), lambda g, place: (g, 0))
    share_rows = SHARE * blocks * width // TILE
    high, low, terms = call(
        product_kernel, "product", 20, (steps,),
        [own_spec, own_spec]
        + [
            pl.BlockSpec((PIECE, blocks, width), lambda g, place, e=e: (lax.rem(place[0] + 2 * g + e, DEPTH), 0, 0))
            for e in range(2)
        ],
        [panel_spec, panel_spec, whole(PEERS, share_rows + TILES * 8, TILE)],
        [bf16(rows, FULL), bf16(rows, FULL), f32(PEERS, share_rows + TILES * 8, TILE)],
        [pltpu.VMEM((FULL, FULL), jnp.float32)],
    )(place, own, other, *in_hbm(matrix, matrix))
    total = jnp.sum(lax.all_to_all(terms, "row", 0, 0), axis=0)
    gram = everywhere(total[share_rows:])
    sums = everywhere(total[:share_rows])

    m, qh, ql = call(
        factor_kernel, "factor", 20, (1,),
        [whole(PEERS, TILES * 8, TILE)] * 2 + [whole(rows, FULL)] * 2,
        [whole(FULL, FULL), whole(rows, FULL), whole(rows, FULL)],
        [f32(FULL, FULL), bf16(rows, FULL), bf16(rows, FULL)],
        [pltpu.VMEM((NB, FULL, TILE), jnp.float32), pltpu.VMEM((NB, TILE, FULL), jnp.float32)],
    )(place, gram, swap_cores(gram), *in_hbm(high, low))

    a_spec = pl.BlockSpec((step, blocks, width), lambda g, place: (g, 0, 0))
    return call(
        remainder_kernel, "remainder", 22, (steps,),
        [panel_spec, panel_spec, a_spec, whole(FULL, FULL), whole(PEERS, share_rows, TILE)],
        [whole(FULL, blocks, width), a_spec],
        [f32(FULL, blocks, width), f32(rows, blocks, width)],
        [pltpu.VMEM((FULL, blocks * width), jnp.bfloat16)] * 2,
    )(place, *in_hbm(qh, ql, matrix), m, sums)


def solution(mesh):
    return jax.shard_map(
        on_device,
        mesh=mesh,
        in_specs=(P("row", None, "col"),),
        out_specs=(P(None, None, "col"), P("row", None, "col")),
        check_vma=False,
    )
```

```python
import jax
import jax.numpy as jnp
from jax import lax
from jax.experimental import pallas as pl
from jax.experimental.pallas import tpu as pltpu
from jax.sharding import PartitionSpec as P

BLOCK = 256
TILE = 128
NB = 4
STRIP = 8
FULL = NB * TILE
PEERS = 16
DEPTH = 8
PIECE = 128
HALF = ((0, 0), (1, 0), (1, 1), (2, 0), (2, 1)), ((2, 2), (3, 0), (3, 1), (3, 2), (3, 3))
HALF_ROWS = len(HALF[0]) * TILE
SHARE = FULL // PEERS
TILES = HALF_ROWS // 8 // PEERS

highest = lax.Precision.HIGHEST
by_rows = ((0,), (0,))
plain = ((1,), (0,))
by_cols = ((1,), (1,))


def mm(a, b, dims):
    return lax.dot_general(a, b, (dims, ((), ())), precision=highest, preferred_element_type=jnp.float32)

def invert_factor(s):
    n = TILE
    rows = lax.broadcasted_iota(jnp.int32, (n, n), 0)
    cols = lax.broadcasted_iota(jnp.int32, (n, n), 1)
    t = jnp.where(rows == cols, 1.0, 0.0).astype(jnp.float32)
    s_done, t_done = [], []
    for k in range(0, n, STRIP):
        top = (k // 8) * 8
        off = k - top
        height = n - top
        sub = lax.broadcasted_iota(jnp.int32, (height, n), 0)
        col = [jnp.broadcast_to(s[:, k + m : k + m + 1], (height, n)) for m in range(STRIP)]
        pivot = [[jnp.broadcast_to(col[j][off + i : off + i + 1, :], (8, n)) for j in range(STRIP)] for i in range(STRIP)]
        srow = [jnp.broadcast_to(s[off + m : off + m + 1, :], (8, n)) for m in range(STRIP)]
        trow = [jnp.broadcast_to(t[off + m : off + m + 1, :], (8, n)) for m in range(STRIP)]
        inv = []
        for m in range(STRIP):
            inv.append(1.0 / pivot[m][m])
            for i in range(m + 1, STRIP):
                low = pivot[i][m] * inv[m]
                for j in range(m + 1, STRIP):
                    if j <= i:
                        pivot[i][j] = pivot[i][j] - low * pivot[j][m]
                srow[i] = srow[i] - low * srow[m]
                trow[i] = trow[i] - low * trow[m]
        def tall(x):
            return jnp.concatenate([x] * (height // 8), axis=0) if height > 8 else x
        factor = []
        for m in range(STRIP):
            f = col[m]
            for j in range(m):
                f = f - factor[j] * tall(pivot[m][j])
            f = f * tall(inv[m])
            factor.append(f)
        for m in range(STRIP):
            f = jnp.where(sub > off + m, factor[m], 0.0)
            s = s - f * tall(srow[m])
            t = t - f * tall(trow[m])
        if off + STRIP == 8:
            s_done.append(s[:8])
            t_done.append(t[:8])
            if height > 8:
                s, t = s[8:], t[8:]
    s = jnp.concatenate(s_done, axis=0)
    t = jnp.concatenate(t_done, axis=0)
    diag = jnp.sum(jnp.where(rows == cols, s, 0.0), axis=1, keepdims=True)
    return t * lax.rsqrt(diag)


def split(x):
    high = x.astype(jnp.bfloat16)
    return high, (x - high.astype(jnp.float32)).astype(jnp.bfloat16)


def one_pass(a, b, dims):
    return lax.dot_general(a, b, (dims, ((), ())), preferred_element_type=jnp.float32)


def three_pass(a, b, dims):
    return one_pass(a[0], b[0], dims) + (one_pass(a[0], b[1], dims) + one_pass(a[1], b[0], dims))


def panel_kernel(matrix_ref, *refs):
    outs, sems = refs[:-1], refs[-1]
    copies = [
        pltpu.make_async_copy(matrix_ref.at[k * PIECE : (k + 1) * PIECE, 0, :], out, sems.at[k]) for k, out in enumerate(outs)
    ]
    for copy in copies:
        copy.start()
    for copy in copies:
        copy.wait()


def product_kernel(place, own_ref, other_ref, a0_ref, a1_ref, high_ref, low_ref, terms_ref, gram_ref):
    start = pl.program_id(0) == 0

    @pl.when(start)
    def _():
        terms_ref[...] = jnp.zeros_like(terms_ref)
        gram_ref[...] = jnp.zeros_like(gram_ref)

    first = place[1] == 0
    own, other = own_ref[...], other_ref[...]
    panel = split(jnp.concatenate([jnp.where(first, own, other), jnp.where(first, other, own)], axis=1))
    high_ref[...], low_ref[...] = panel
    gram_ref[...] += three_pass(panel, panel, by_rows)
    for l in range(a0_ref.shape[1]):
        a = split(jnp.concatenate([a0_ref[:, l, :], a1_ref[:, l, :]], axis=0))
        part = three_pass(panel, a, by_rows)
        for r in range(PEERS):
            for e in range(BLOCK // TILE):
                spot = slice((l * BLOCK // TILE + e) * SHARE, (l * BLOCK // TILE + e + 1) * SHARE)
                terms_ref[r, spot, :] += part[r * SHARE : (r + 1) * SHARE, e * TILE : (e + 1) * TILE]

    @pl.when(pl.program_id(0) == pl.num_programs(0) - 1)
    def _():
        for n in range(HALF_ROWS // 8):
            (i, j), (p, q) = (half[n // 16] for half in HALF)
            top = n % 16 * 8
            here = gram_ref[i * TILE + top : i * TILE + top + 8, j * TILE : (j + 1) * TILE]
            there = gram_ref[p * TILE + top : p * TILE + top + 8, q * TILE : (q + 1) * TILE]
            spot = terms_ref.shape[1] + (n % TILES - TILES) * 8
            terms_ref[n // TILES, spot : spot + 8, :] = jnp.where(first, here, there)


def total_kernel(place, terms_ref, gram_ref, sums_ref):
    peers, split_row = sums_ref.shape[:2]
    total = terms_ref[0]
    for r in range(1, peers):
        total = total + terms_ref[r]
    for r in range(peers):
        sums_ref[r] = total[:split_row]
        gram_ref[r] = total[split_row:]


def factor_kernel(place, own_ref, other_ref, high_ref, low_ref, m_ref, qh_ref, ql_ref, s_ref, t_ref):
    first = place[1] == 0
    s_ref[...] = jnp.zeros_like(s_ref)
    t_ref[...] = jnp.zeros_like(t_ref)
    for n in range(HALF_ROWS // 8):
        (i, j), (p, q) = (half[n // 16] for half in HALF)
        top = n % 16 * 8
        spot = slice(n % TILES * 8, n % TILES * 8 + 8)
        own = own_ref[n // TILES, spot, :]
        other = other_ref[n // TILES, spot, :]
        s_ref[j, i * TILE + top : i * TILE + top + 8, :] = jnp.where(first, own, other)
        s_ref[q, p * TILE + top : p * TILE + top + 8, :] = jnp.where(first, other, own)

    def update(j, i, k):
        s_ref[k, i * TILE : (i + 1) * TILE, :] -= mm(low[i], low[k], by_cols)

    for j in range(NB):
        d = j * TILE
        mj = invert_factor(s_ref[j, d : d + TILE, :])
        if j:
            done = j - 1
            for i in range(j, NB):
                t_ref[i, :, :d] -= mm(low[i], m_ref[done * TILE : d, :d], plain)
                for k in range(j, i + 1):
                    if i > j:
                        update(done, i, k)
            m_ref[d : d + TILE, :d] = mm(mj, t_ref[j, :, :d], plain)
        m_ref[d : d + TILE, d : d + TILE] = mj
        if j + 1 < NB:
            m_ref[d : d + TILE, d + TILE :] = jnp.zeros((TILE, FULL - d - TILE), jnp.float32)
            column = mm(s_ref[j, d + TILE :, :], mj, by_cols)
            low = {i: column[(i - j - 1) * TILE : (i - j) * TILE] for i in range(j + 1, NB)}
            update(j, j + 1, j + 1)

    factor = split(m_ref[...])
    step = 2 * PIECE
    for g in range(0, DEPTH, 2):
        window = slice(g * PIECE, g * PIECE + step)
        q = split(three_pass((high_ref[window], low_ref[window]), factor, by_cols))
        for e in range(2):
            spot = pl.ds(pl.multiple_of(lax.rem(place[0] + g + e, DEPTH) * PIECE, PIECE), PIECE)
            qh_ref[spot, :] = q[0][e * PIECE : (e + 1) * PIECE]
            ql_ref[spot, :] = q[1][e * PIECE : (e + 1) * PIECE]


def remainder_kernel(place, qh_ref, ql_ref, a_ref, m_ref, w_ref, coeff_ref, out_ref, ch_ref, cl_ref):
    width = a_ref.shape[2]
    each = width // TILE

    @pl.when(pl.program_id(0) == 0)
    def _():
        factor = split(m_ref[...])
        for l in range(coeff_ref.shape[1]):
            tiles = [w_ref[:, t * SHARE : (t + 1) * SHARE, :].reshape(FULL, TILE) for t in range(l * each, (l + 1) * each)]
            coeffs = three_pass(factor, split(jnp.concatenate(tiles, axis=1)), plain)
            coeff_ref[:, l, :] = coeffs
            window = slice(l * width, (l + 1) * width)
            ch_ref[:, window], cl_ref[:, window] = split(coeffs)

    q = qh_ref[...], ql_ref[...]
    for l in range(a_ref.shape[1]):
        window = slice(l * width, (l + 1) * width)
        out_ref[:, l, :] = a_ref[:, l, :] - three_pass(q, (ch_ref[:, window], cl_ref[:, window]), plain)


def call(kernel, name, mib, grid, ins, outs, out_shape, scratch=()):
    return pl.pallas_call(
        kernel,
        out_shape=out_shape,
        grid_spec=pltpu.PrefetchScalarGridSpec(
            num_scalar_prefetch=1, grid=grid, in_specs=ins, out_specs=outs, scratch_shapes=scratch
        ),
        compiler_params=pltpu.CompilerParams(vmem_limit_bytes=mib << 20),
        name=name,
    )


def whole(*shape):
    return pl.BlockSpec(shape, lambda g, place: (0,) * len(shape))


def f32(*shape):
    return jax.ShapeDtypeStruct(shape, jnp.float32)


def bf16(*shape):
    return pltpu.HBM(shape, jnp.bfloat16)


def in_hbm(*arrays):
    return [pltpu.with_memory_space_constraint(x, pltpu.HBM) for x in arrays]


def shift(x, axis, by):
    return lax.ppermute(x, axis, [(i, (i + by) % PEERS) for i in range(PEERS)])


def exchange(x):
    return lax.all_to_all(x, "row", 0, 0)


def swap_cores(x):
    return lax.ppermute(x, "col", [(i, i ^ 1) for i in range(PEERS)])


def share_panel(mine, z):
    own = jnp.where(z == 0, mine[0], jnp.zeros((PIECE, BLOCK), jnp.float32))
    for k in (1, 7, 2, 6, 4, 3, 5):
        own = own + lax.ppermute(mine[k], "col", [(0, 2 * k), (1, 2 * k + 1)])
    own = lax.optimization_barrier(own)
    up, down = [own], [own]
    for _ in range(DEPTH // 2 - 1):
        up.append(shift(up[-1], "col", 2))
        down.append(shift(down[-1], "col", -2))
    half = PIECE // 2
    far = [shift(up[-1][:half], "col", 2), shift(down[-1][half:], "col", -2)]
    return jnp.concatenate(down + far + up[:0:-1], axis=0)


def on_device(matrix):
    rows, blocks, width = matrix.shape
    col = lax.axis_index("col")
    z, core, row = col // 2, col % 2, lax.axis_index("row")
    place = jnp.stack([z, core, row]).astype(jnp.int32)

    mine = pl.pallas_call(
        panel_kernel,
        in_specs=[pl.BlockSpec(memory_space=pl.ANY)],
        out_specs=[pl.BlockSpec(memory_space=pltpu.VMEM)] * DEPTH,
        out_shape=[f32(PIECE, width)] * DEPTH,
        scratch_shapes=[pltpu.SemaphoreType.DMA((DEPTH,))],
        name="panel",
    )(*in_hbm(matrix))
    own = share_panel(mine, z)
    other = swap_cores(own)

    step = 2 * PIECE
    steps = rows // step
    own_spec = pl.BlockSpec((step, BLOCK), lambda g, place: (g, 0))
    panel_spec = pl.BlockSpec((step, FULL), lambda g, place: (g, 0))
    share_rows = SHARE * blocks * width // TILE
    high, low, terms = call(
        product_kernel, "product", 20, (steps,),
        [own_spec, own_spec]
        + [
            pl.BlockSpec((PIECE, blocks, width), lambda g, place, e=e: (lax.rem(place[0] + 2 * g + e, DEPTH), 0, 0))
            for e in range(2)
        ],
        [panel_spec, panel_spec, whole(PEERS, share_rows + TILES * 8, TILE)],
        [bf16(rows, FULL), bf16(rows, FULL), f32(PEERS, share_rows + TILES * 8, TILE)],
        [pltpu.VMEM((FULL, FULL), jnp.float32)],
    )(place, own, other, *in_hbm(matrix, matrix))
    gram_rows = TILES * 8
    gram, sums = call(
        total_kernel, "total", 16, (1,),
        [whole(PEERS, share_rows + gram_rows, TILE)],
        [whole(PEERS, gram_rows, TILE), whole(PEERS, share_rows, TILE)],
        [f32(PEERS, gram_rows, TILE), pltpu.HBM((PEERS, share_rows, TILE), jnp.float32)],
    )(place, exchange(terms))
    gram = exchange(gram)
    sums = exchange(sums)

    m, qh, ql = call(
        factor_kernel, "factor", 20, (1,),
        [whole(PEERS, TILES * 8, TILE)] * 2 + [whole(rows, FULL)] * 2,
        [whole(FULL, FULL), whole(rows, FULL), whole(rows, FULL)],
        [f32(FULL, FULL), bf16(rows, FULL), bf16(rows, FULL)],
        [pltpu.VMEM((NB, FULL, TILE), jnp.float32), pltpu.VMEM((NB, TILE, FULL), jnp.float32)],
    )(place, gram, swap_cores(gram), *in_hbm(high, low))

    a_spec = pl.BlockSpec((step, blocks, width), lambda g, place: (g, 0, 0))
    return call(
        remainder_kernel, "remainder", 22, (steps,),
        [panel_spec, panel_spec, a_spec, whole(FULL, FULL), whole(PEERS, share_rows, TILE)],
        [whole(FULL, blocks, width), a_spec],
        [f32(FULL, blocks, width), f32(rows, blocks, width)],
        [pltpu.VMEM((FULL, blocks * width), jnp.bfloat16)] * 2,
    )(place, *in_hbm(qh, ql, matrix), m, sums)


def solution(mesh):
    return jax.shard_map(
        on_device,
        mesh=mesh,
        in_specs=(P("row", None, "col"),),
        out_specs=(P(None, None, "col"), P("row", None, "col")),
        check_vma=False,
    )
```

```python
import jax
import jax.numpy as jnp
from jax import lax
from jax.experimental import pallas as pl
from jax.experimental.pallas import tpu as pltpu
from jax.sharding import PartitionSpec as P

BLOCK = 256
TILE = 128
NB = 4
STRIP = 8
FULL = NB * TILE
PEERS = 16
DEPTH = 8
PIECE = 128
HALF = ((0, 0), (1, 0), (1, 1), (2, 0), (2, 1)), ((2, 2), (3, 0), (3, 1), (3, 2), (3, 3))
HALF_ROWS = len(HALF[0]) * TILE
SHARE = FULL // PEERS
TILES = HALF_ROWS // 8 // PEERS

highest = lax.Precision.HIGHEST
by_rows = ((0,), (0,))
plain = ((1,), (0,))
by_cols = ((1,), (1,))


def mm(a, b, dims):
    return lax.dot_general(a, b, (dims, ((), ())), precision=highest, preferred_element_type=jnp.float32)

def invert_factor(s):
    n = TILE
    rows = lax.broadcasted_iota(jnp.int32, (n, n), 0)
    cols = lax.broadcasted_iota(jnp.int32, (n, n), 1)
    t = jnp.where(rows == cols, 1.0, 0.0).astype(jnp.float32)
    s_done, t_done = [], []
    for k in range(0, n, STRIP):
        top = (k // 8) * 8
        off = k - top
        height = n - top
        sub = lax.broadcasted_iota(jnp.int32, (height, n), 0)
        col = [jnp.broadcast_to(s[:, k + m : k + m + 1], (height, n)) for m in range(STRIP)]
        pivot = [[jnp.broadcast_to(col[j][off + i : off + i + 1, :], (8, n)) for j in range(STRIP)] for i in range(STRIP)]
        srow = [jnp.broadcast_to(s[off + m : off + m + 1, :], (8, n)) for m in range(STRIP)]
        trow = [jnp.broadcast_to(t[off + m : off + m + 1, :], (8, n)) for m in range(STRIP)]
        inv = []
        for m in range(STRIP):
            inv.append(1.0 / pivot[m][m])
            for i in range(m + 1, STRIP):
                low = pivot[i][m] * inv[m]
                for j in range(m + 1, STRIP):
                    if j <= i:
                        pivot[i][j] = pivot[i][j] - low * pivot[j][m]
                srow[i] = srow[i] - low * srow[m]
                trow[i] = trow[i] - low * trow[m]
        def tall(x):
            return jnp.concatenate([x] * (height // 8), axis=0) if height > 8 else x
        factor = []
        for m in range(STRIP):
            f = col[m]
            for j in range(m):
                f = f - factor[j] * tall(pivot[m][j])
            f = f * tall(inv[m])
            factor.append(f)
        for m in range(STRIP):
            f = jnp.where(sub > off + m, factor[m], 0.0)
            s = s - f * tall(srow[m])
            t = t - f * tall(trow[m])
        if off + STRIP == 8:
            s_done.append(s[:8])
            t_done.append(t[:8])
            if height > 8:
                s, t = s[8:], t[8:]
    s = jnp.concatenate(s_done, axis=0)
    t = jnp.concatenate(t_done, axis=0)
    diag = jnp.sum(jnp.where(rows == cols, s, 0.0), axis=1, keepdims=True)
    return t * lax.rsqrt(diag)


def split(x):
    high = x.astype(jnp.bfloat16)
    return high, (x - high.astype(jnp.float32)).astype(jnp.bfloat16)


def one_pass(a, b, dims):
    return lax.dot_general(a, b, (dims, ((), ())), preferred_element_type=jnp.float32)


def three_pass(a, b, dims):
    return one_pass(a[0], b[0], dims) + (one_pass(a[0], b[1], dims) + one_pass(a[1], b[0], dims))


def panel_kernel(matrix_ref, *refs):
    outs, sems = refs[:-1], refs[-1]
    copies = [
        pltpu.make_async_copy(matrix_ref.at[k * PIECE : (k + 1) * PIECE, 0, :], out, sems.at[k]) for k, out in enumerate(outs)
    ]
    for copy in copies:
        copy.start()
    for copy in copies:
        copy.wait()


def product_kernel(place, own_ref, other_ref, a0_ref, a1_ref, high_ref, low_ref, terms_ref, gram_ref):
    start = pl.program_id(0) == 0

    @pl.when(start)
    def _():
        terms_ref[...] = jnp.zeros_like(terms_ref)
        gram_ref[...] = jnp.zeros_like(gram_ref)

    first = place[1] == 0
    own, other = own_ref[...], other_ref[...]
    panel = split(jnp.concatenate([jnp.where(first, own, other), jnp.where(first, other, own)], axis=1))
    high_ref[...], low_ref[...] = panel
    gram_ref[...] += three_pass(panel, panel, by_rows) + one_pass(panel[1], panel[1], by_rows)
    for l in range(a0_ref.shape[1]):
        a = split(jnp.concatenate([a0_ref[:, l, :], a1_ref[:, l, :]], axis=0))
        part = three_pass(panel, a, by_rows)
        for r in range(PEERS):
            for e in range(BLOCK // TILE):
                spot = slice((l * BLOCK // TILE + e) * SHARE, (l * BLOCK // TILE + e + 1) * SHARE)
                terms_ref[r, spot, :] += part[r * SHARE : (r + 1) * SHARE, e * TILE : (e + 1) * TILE]

    @pl.when(pl.program_id(0) == pl.num_programs(0) - 1)
    def _():
        for n in range(HALF_ROWS // 8):
            (i, j), (p, q) = (half[n // 16] for half in HALF)
            top = n % 16 * 8
            here = gram_ref[i * TILE + top : i * TILE + top + 8, j * TILE : (j + 1) * TILE]
            there = gram_ref[p * TILE + top : p * TILE + top + 8, q * TILE : (q + 1) * TILE]
            spot = terms_ref.shape[1] + (n % TILES - TILES) * 8
            terms_ref[n // TILES, spot : spot + 8, :] = jnp.where(first, here, there)


def total_kernel(place, terms_ref, gram_ref, sums_ref):
    peers, split_row = sums_ref.shape[:2]
    total = terms_ref[0]
    for r in range(1, peers):
        total = total + terms_ref[r]
    for r in range(peers):
        sums_ref[r] = total[:split_row]
        gram_ref[r] = total[split_row:]


def factor_kernel(place, own_ref, other_ref, high_ref, low_ref, m_ref, qh_ref, ql_ref, s_ref, t_ref):
    first = place[1] == 0
    s_ref[...] = jnp.zeros_like(s_ref)
    t_ref[...] = jnp.zeros_like(t_ref)
    for n in range(HALF_ROWS // 8):
        (i, j), (p, q) = (half[n // 16] for half in HALF)
        top = n % 16 * 8
        spot = slice(n % TILES * 8, n % TILES * 8 + 8)
        own = own_ref[n // TILES, spot, :]
        other = other_ref[n // TILES, spot, :]
        s_ref[j, i * TILE + top : i * TILE + top + 8, :] = jnp.where(first, own, other)
        s_ref[q, p * TILE + top : p * TILE + top + 8, :] = jnp.where(first, other, own)

    def update(j, i, k):
        s_ref[k, i * TILE : (i + 1) * TILE, :] -= mm(low[i], low[k], by_cols)

    for j in range(NB):
        d = j * TILE
        mj = invert_factor(s_ref[j, d : d + TILE, :])
        if j:
            done = j - 1
            for i in range(j, NB):
                t_ref[i, :, :d] -= three_pass(split(low[i]), split(m_ref[done * TILE : d, :d]), plain)
                for k in range(j, i + 1):
                    if i > j:
                        update(done, i, k)
            m_ref[d : d + TILE, :d] = three_pass(split(mj), split(t_ref[j, :, :d]), plain)
        m_ref[d : d + TILE, d : d + TILE] = mj
        if j + 1 < NB:
            m_ref[d : d + TILE, d + TILE :] = jnp.zeros((TILE, FULL - d - TILE), jnp.float32)
            column = mm(s_ref[j, d + TILE :, :], mj, by_cols)
            low = {i: column[(i - j - 1) * TILE : (i - j) * TILE] for i in range(j + 1, NB)}
            update(j, j + 1, j + 1)

    factor = split(m_ref[...])
    step = 2 * PIECE
    for g in range(0, DEPTH, 2):
        window = slice(g * PIECE, g * PIECE + step)
        q = split(three_pass((high_ref[window], low_ref[window]), factor, by_cols))
        for e in range(2):
            spot = pl.ds(pl.multiple_of(lax.rem(place[0] + g + e, DEPTH) * PIECE, PIECE), PIECE)
            qh_ref[spot, :] = q[0][e * PIECE : (e + 1) * PIECE]
            ql_ref[spot, :] = q[1][e * PIECE : (e + 1) * PIECE]


def remainder_kernel(place, qh_ref, ql_ref, a_ref, m_ref, w_ref, coeff_ref, out_ref, ch_ref, cl_ref, c_ref, sem):
    width = a_ref.shape[2]
    each = width // TILE
    copy = pltpu.make_async_copy(c_ref, coeff_ref, sem)

    @pl.when(pl.program_id(0) == 0)
    def _():
        factor = split(m_ref[...])
        for l in range(c_ref.shape[1]):
            tiles = [w_ref[:, t * SHARE : (t + 1) * SHARE, :].reshape(FULL, TILE) for t in range(l * each, (l + 1) * each)]
            coeffs = three_pass(factor, split(jnp.concatenate(tiles, axis=1)), plain)
            c_ref[:, l, :] = coeffs
            window = slice(l * width, (l + 1) * width)
            ch_ref[:, window], cl_ref[:, window] = split(coeffs)
        copy.start()

    q = qh_ref[...], ql_ref[...]
    for l in range(a_ref.shape[1]):
        window = slice(l * width, (l + 1) * width)
        out_ref[:, l, :] = a_ref[:, l, :] - three_pass(q, (ch_ref[:, window], cl_ref[:, window]), plain)

    @pl.when(pl.program_id(0) == pl.num_programs(0) - 1)
    def _():
        copy.wait()


def call(kernel, name, mib, grid, ins, outs, out_shape, scratch=()):
    return pl.pallas_call(
        kernel,
        out_shape=out_shape,
        grid_spec=pltpu.PrefetchScalarGridSpec(
            num_scalar_prefetch=1, grid=grid, in_specs=ins, out_specs=outs, scratch_shapes=scratch
        ),
        compiler_params=pltpu.CompilerParams(vmem_limit_bytes=mib << 20),
        name=name,
    )


def whole(*shape):
    return pl.BlockSpec(shape, lambda g, place: (0,) * len(shape))


def f32(*shape):
    return jax.ShapeDtypeStruct(shape, jnp.float32)


def bf16(*shape):
    return pltpu.HBM(shape, jnp.bfloat16)


def in_hbm(*arrays):
    return [pltpu.with_memory_space_constraint(x, pltpu.HBM) for x in arrays]


def shift(x, axis, by):
    return lax.ppermute(x, axis, [(i, (i + by) % PEERS) for i in range(PEERS)])


def exchange(x):
    return lax.all_to_all(x, "row", 0, 0)


def swap_cores(x):
    return lax.ppermute(x, "col", [(i, i ^ 1) for i in range(PEERS)])


def share_panel(mine, z):
    own = jnp.where(z == 0, mine[0], jnp.zeros((PIECE, BLOCK), jnp.float32))
    for k in (1, 7, 2, 6, 4, 3, 5):
        own = own + lax.ppermute(mine[k], "col", [(0, 2 * k), (1, 2 * k + 1)])
    own = lax.optimization_barrier(own)
    up, down = [own], [own]
    for _ in range(DEPTH // 2 - 1):
        up.append(shift(up[-1], "col", 2))
        down.append(shift(down[-1], "col", -2))
    half = PIECE // 2
    far = [shift(up[-1][:half], "col", 2), shift(down[-1][half:], "col", -2)]
    return jnp.concatenate(down + far + up[:0:-1], axis=0)


def on_device(matrix):
    rows, blocks, width = matrix.shape
    col = lax.axis_index("col")
    z, core, row = col // 2, col % 2, lax.axis_index("row")
    place = jnp.stack([z, core, row]).astype(jnp.int32)

    mine = pl.pallas_call(
        panel_kernel,
        in_specs=[pl.BlockSpec(memory_space=pl.ANY)],
        out_specs=[pl.BlockSpec(memory_space=pltpu.VMEM)] * DEPTH,
        out_shape=[f32(PIECE, width)] * DEPTH,
        scratch_shapes=[pltpu.SemaphoreType.DMA((DEPTH,))],
        name="panel",
    )(*in_hbm(matrix))
    own = share_panel(mine, z)
    other = swap_cores(own)

    step = 2 * PIECE
    steps = rows // step
    own_spec = pl.BlockSpec((step, BLOCK), lambda g, place: (g, 0))
    panel_spec = pl.BlockSpec((step, FULL), lambda g, place: (g, 0))
    share_rows = SHARE * blocks * width // TILE
    high, low, terms = call(
        product_kernel, "product", 20, (steps,),
        [own_spec, own_spec]
        + [
            pl.BlockSpec((PIECE, blocks, width), lambda g, place, e=e: (lax.rem(place[0] + 2 * g + e, DEPTH), 0, 0))
            for e in range(2)
        ],
        [panel_spec, panel_spec, whole(PEERS, share_rows + TILES * 8, TILE)],
        [bf16(rows, FULL), bf16(rows, FULL), f32(PEERS, share_rows + TILES * 8, TILE)],
        [pltpu.VMEM((FULL, FULL), jnp.float32)],
    )(place, own, other, *in_hbm(matrix, matrix))
    gram_rows = TILES * 8
    gram, sums = call(
        total_kernel, "total", 16, (1,),
        [whole(PEERS, share_rows + gram_rows, TILE)],
        [whole(PEERS, gram_rows, TILE), whole(PEERS, share_rows, TILE)],
        [f32(PEERS, gram_rows, TILE), pltpu.HBM((PEERS, share_rows, TILE), jnp.float32)],
    )(place, exchange(terms))
    gram = exchange(gram)
    sums = exchange(sums)

    m, qh, ql = call(
        factor_kernel, "factor", 20, (1,),
        [whole(PEERS, TILES * 8, TILE)] * 2 + [whole(rows, FULL)] * 2,
        [whole(FULL, FULL), whole(rows, FULL), whole(rows, FULL)],
        [f32(FULL, FULL), bf16(rows, FULL), bf16(rows, FULL)],
        [pltpu.VMEM((NB, FULL, TILE), jnp.float32), pltpu.VMEM((NB, TILE, FULL), jnp.float32)],
    )(place, gram, swap_cores(gram), *in_hbm(high, low))

    a_spec = pl.BlockSpec((step, blocks, width), lambda g, place: (g, 0, 0))
    return call(
        remainder_kernel, "remainder", 22, (steps,),
        [panel_spec, panel_spec, a_spec, whole(FULL, FULL), whole(PEERS, share_rows, TILE)],
        [pl.BlockSpec(memory_space=pl.ANY), a_spec],
        [f32(FULL, blocks, width), f32(rows, blocks, width)],
        [pltpu.VMEM((FULL, blocks * width), jnp.bfloat16)] * 2
        + [pltpu.VMEM((FULL, blocks, width), jnp.float32), pltpu.SemaphoreType.DMA],
    )(place, *in_hbm(qh, ql, matrix), m, sums)


def solution(mesh):
    return jax.shard_map(
        on_device,
        mesh=mesh,
        in_specs=(P("row", None, "col"),),
        out_specs=(P(None, None, "col"), P("row", None, "col")),
        check_vma=False,
    )
```

```python
import jax
import jax.numpy as jnp
from jax import lax
from jax.experimental import pallas as pl
from jax.experimental.pallas import tpu as pltpu
from jax.sharding import PartitionSpec as P

BLOCK = 256
TILE = 128
NB = 4
STRIP = 8
FULL = NB * TILE
PEERS = 16
DEPTH = 8
PIECE = 128
NEAR = (1, 7)
FAR = (2, 6, 4, 3, 5, 0)
HALF = ((0, 0), (1, 0), (1, 1), (2, 0), (2, 1)), ((2, 2), (3, 0), (3, 1), (3, 2), (3, 3))
HALF_ROWS = len(HALF[0]) * TILE
SHARE = FULL // PEERS
TILES = HALF_ROWS // 8 // PEERS

highest = lax.Precision.HIGHEST
by_rows = ((0,), (0,))
plain = ((1,), (0,))
by_cols = ((1,), (1,))


def mm(a, b, dims):
    return lax.dot_general(a, b, (dims, ((), ())), precision=highest, preferred_element_type=jnp.float32)

def invert_factor(s):
    n = TILE
    rows = lax.broadcasted_iota(jnp.int32, (n, n), 0)
    cols = lax.broadcasted_iota(jnp.int32, (n, n), 1)
    t = jnp.where(rows == cols, 1.0, 0.0).astype(jnp.float32)
    s_done, t_done = [], []
    for k in range(0, n, STRIP):
        top = (k // 8) * 8
        off = k - top
        height = n - top
        sub = lax.broadcasted_iota(jnp.int32, (height, n), 0)
        col = [jnp.broadcast_to(s[:, k + m : k + m + 1], (height, n)) for m in range(STRIP)]
        pivot = [[jnp.broadcast_to(col[j][off + i : off + i + 1, :], (8, n)) for j in range(STRIP)] for i in range(STRIP)]
        srow = [jnp.broadcast_to(s[off + m : off + m + 1, :], (8, n)) for m in range(STRIP)]
        trow = [jnp.broadcast_to(t[off + m : off + m + 1, :], (8, n)) for m in range(STRIP)]
        inv = []
        for m in range(STRIP):
            inv.append(1.0 / pivot[m][m])
            for i in range(m + 1, STRIP):
                low = pivot[i][m] * inv[m]
                for j in range(m + 1, STRIP):
                    if j <= i:
                        pivot[i][j] = pivot[i][j] - low * pivot[j][m]
                srow[i] = srow[i] - low * srow[m]
                trow[i] = trow[i] - low * trow[m]
        def tall(x):
            return jnp.concatenate([x] * (height // 8), axis=0) if height > 8 else x
        factor = []
        for m in range(STRIP):
            f = col[m]
            for j in range(m):
                f = f - factor[j] * tall(pivot[m][j])
            f = f * tall(inv[m])
            factor.append(f)
        for m in range(STRIP):
            f = jnp.where(sub > off + m, factor[m], 0.0)
            s = s - f * tall(srow[m])
            t = t - f * tall(trow[m])
        if off + STRIP == 8:
            s_done.append(s[:8])
            t_done.append(t[:8])
            if height > 8:
                s, t = s[8:], t[8:]
    s = jnp.concatenate(s_done, axis=0)
    t = jnp.concatenate(t_done, axis=0)
    diag = jnp.sum(jnp.where(rows == cols, s, 0.0), axis=1, keepdims=True)
    return t * lax.rsqrt(diag)


def split(x):
    high = x.astype(jnp.bfloat16)
    return high, (x - high.astype(jnp.float32)).astype(jnp.bfloat16)


def one_pass(a, b, dims):
    return lax.dot_general(a, b, (dims, ((), ())), preferred_element_type=jnp.float32)


def three_pass(a, b, dims):
    return one_pass(a[0], b[0], dims) + (one_pass(a[0], b[1], dims) + one_pass(a[1], b[0], dims))


def panel_rows(matrix, pieces):
    rows, blocks, width = matrix.shape

    def kernel(matrix_ref, *refs):
        copies = [
            pltpu.make_async_copy(matrix_ref.at[k * PIECE : (k + 1) * PIECE, 0, :], out, refs[-1].at[i])
            for i, (k, out) in enumerate(zip(pieces, refs[:-1]))
        ]
        for copy in copies:
            copy.start()
        for copy in copies:
            copy.wait()

    outs = pl.pallas_call(
        kernel,
        in_specs=[pl.BlockSpec(memory_space=pl.ANY)],
        out_specs=[pl.BlockSpec(memory_space=pltpu.VMEM)] * len(pieces),
        out_shape=[f32(PIECE, width)] * len(pieces),
        scratch_shapes=[pltpu.SemaphoreType.DMA((len(pieces),))],
        name="panel",
    )(*in_hbm(matrix))
    return dict(zip(pieces, outs))


def product_kernel(place, own_ref, other_ref, a0_ref, a1_ref, high_ref, low_ref, terms_ref, gram_ref):
    start = pl.program_id(0) == 0

    @pl.when(start)
    def _():
        terms_ref[...] = jnp.zeros_like(terms_ref)
        gram_ref[...] = jnp.zeros_like(gram_ref)

    first = place[1] == 0
    own, other = own_ref[...], other_ref[...]
    panel = split(jnp.concatenate([jnp.where(first, own, other), jnp.where(first, other, own)], axis=1))
    high_ref[...], low_ref[...] = panel
    gram_ref[...] += three_pass(panel, panel, by_rows) + one_pass(panel[1], panel[1], by_rows)
    for l in range(a0_ref.shape[1]):
        a = split(jnp.concatenate([a0_ref[:, l, :], a1_ref[:, l, :]], axis=0))
        part = three_pass(panel, a, by_rows)
        for r in range(PEERS):
            for e in range(BLOCK // TILE):
                spot = slice((l * BLOCK // TILE + e) * SHARE, (l * BLOCK // TILE + e + 1) * SHARE)
                terms_ref[r, spot, :] += part[r * SHARE : (r + 1) * SHARE, e * TILE : (e + 1) * TILE]

    @pl.when(pl.program_id(0) == pl.num_programs(0) - 1)
    def _():
        for n in range(HALF_ROWS // 8):
            (i, j), (p, q) = (half[n // 16] for half in HALF)
            top = n % 16 * 8
            here = gram_ref[i * TILE + top : i * TILE + top + 8, j * TILE : (j + 1) * TILE]
            there = gram_ref[p * TILE + top : p * TILE + top + 8, q * TILE : (q + 1) * TILE]
            spot = terms_ref.shape[1] + (n % TILES - TILES) * 8
            terms_ref[n // TILES, spot : spot + 8, :] = jnp.where(first, here, there)


def total_kernel(place, terms_ref, gram_ref, sums_ref):
    peers, split_row = sums_ref.shape[:2]
    total = terms_ref[0]
    for r in range(1, peers):
        total = total + terms_ref[r]
    for r in range(peers):
        sums_ref[r] = total[:split_row]
        gram_ref[r] = total[split_row:]


def factor_kernel(place, own_ref, other_ref, high_ref, low_ref, m_ref, qh_ref, ql_ref, s_ref, t_ref):
    first = place[1] == 0
    s_ref[...] = jnp.zeros_like(s_ref)
    t_ref[...] = jnp.zeros_like(t_ref)
    for n in range(HALF_ROWS // 8):
        (i, j), (p, q) = (half[n // 16] for half in HALF)
        top = n % 16 * 8
        spot = slice(n % TILES * 8, n % TILES * 8 + 8)
        own = own_ref[n // TILES, spot, :]
        other = other_ref[n // TILES, spot, :]
        s_ref[j, i * TILE + top : i * TILE + top + 8, :] = jnp.where(first, own, other)
        s_ref[q, p * TILE + top : p * TILE + top + 8, :] = jnp.where(first, other, own)

    def update(j, i, k):
        s_ref[k, i * TILE : (i + 1) * TILE, :] -= mm(low[i], low[k], by_cols)

    for j in range(NB):
        d = j * TILE
        mj = invert_factor(s_ref[j, d : d + TILE, :])
        if j:
            done = j - 1
            for i in range(j, NB):
                t_ref[i, :, :d] -= three_pass(split(low[i]), split(m_ref[done * TILE : d, :d]), plain)
                for k in range(j, i + 1):
                    if i > j:
                        update(done, i, k)
            m_ref[d : d + TILE, :d] = three_pass(split(mj), split(t_ref[j, :, :d]), plain)
        m_ref[d : d + TILE, d : d + TILE] = mj
        if j + 1 < NB:
            m_ref[d : d + TILE, d + TILE :] = jnp.zeros((TILE, FULL - d - TILE), jnp.float32)
            column = mm(s_ref[j, d + TILE :, :], mj, by_cols)
            low = {i: column[(i - j - 1) * TILE : (i - j) * TILE] for i in range(j + 1, NB)}
            update(j, j + 1, j + 1)

    factor = split(m_ref[...])
    step = 2 * PIECE
    for g in range(0, DEPTH, 2):
        window = slice(g * PIECE, g * PIECE + step)
        q = split(three_pass((high_ref[window], low_ref[window]), factor, by_cols))
        for e in range(2):
            spot = pl.ds(pl.multiple_of(lax.rem(place[0] + g + e, DEPTH) * PIECE, PIECE), PIECE)
            qh_ref[spot, :] = q[0][e * PIECE : (e + 1) * PIECE]
            ql_ref[spot, :] = q[1][e * PIECE : (e + 1) * PIECE]


def remainder_kernel(place, qh_ref, ql_ref, a_ref, m_ref, w_ref, coeff_ref, out_ref, ch_ref, cl_ref, c_ref, sem):
    width = a_ref.shape[2]
    each = width // TILE
    copy = pltpu.make_async_copy(c_ref, coeff_ref, sem)

    @pl.when(pl.program_id(0) == 0)
    def _():
        factor = split(m_ref[...])
        for l in range(c_ref.shape[1]):
            tiles = [w_ref[:, t * SHARE : (t + 1) * SHARE, :].reshape(FULL, TILE) for t in range(l * each, (l + 1) * each)]
            coeffs = three_pass(factor, split(jnp.concatenate(tiles, axis=1)), plain)
            c_ref[:, l, :] = coeffs
            window = slice(l * width, (l + 1) * width)
            ch_ref[:, window], cl_ref[:, window] = split(coeffs)
        copy.start()

    q = qh_ref[...], ql_ref[...]
    for l in range(a_ref.shape[1]):
        window = slice(l * width, (l + 1) * width)
        out_ref[:, l, :] = a_ref[:, l, :] - three_pass(q, (ch_ref[:, window], cl_ref[:, window]), plain)

    @pl.when(pl.program_id(0) == pl.num_programs(0) - 1)
    def _():
        copy.wait()


def call(kernel, name, mib, grid, ins, outs, out_shape, scratch=()):
    return pl.pallas_call(
        kernel,
        out_shape=out_shape,
        grid_spec=pltpu.PrefetchScalarGridSpec(
            num_scalar_prefetch=1, grid=grid, in_specs=ins, out_specs=outs, scratch_shapes=scratch
        ),
        compiler_params=pltpu.CompilerParams(vmem_limit_bytes=mib << 20),
        name=name,
    )


def whole(*shape):
    return pl.BlockSpec(shape, lambda g, place: (0,) * len(shape))


def f32(*shape):
    return jax.ShapeDtypeStruct(shape, jnp.float32)


def bf16(*shape):
    return pltpu.HBM(shape, jnp.bfloat16)


def in_hbm(*arrays):
    return [pltpu.with_memory_space_constraint(x, pltpu.HBM) for x in arrays]


def shift(x, axis, by):
    return lax.ppermute(x, axis, [(i, (i + by) % PEERS) for i in range(PEERS)])


def exchange(x):
    return lax.all_to_all(x, "row", 0, 0)


def swap_cores(x):
    return lax.ppermute(x, "col", [(i, i ^ 1) for i in range(PEERS)])


def share_panel(mine, z):
    own = jnp.where(z == 0, mine[0], jnp.zeros((PIECE, BLOCK), jnp.float32))
    for k in NEAR + FAR[:-1]:
        own = own + lax.ppermute(mine[k], "col", [(0, 2 * k), (1, 2 * k + 1)])
    own = lax.optimization_barrier(own)
    up, down = [own], [own]
    for _ in range(DEPTH // 2 - 1):
        up.append(shift(up[-1], "col", 2))
        down.append(shift(down[-1], "col", -2))
    half = PIECE // 2
    far = [shift(up[-1][:half], "col", 2), shift(down[-1][half:], "col", -2)]
    return jnp.concatenate(down + far + up[:0:-1], axis=0)


def on_device(matrix):
    rows, blocks, width = matrix.shape
    col = lax.axis_index("col")
    z, core, row = col // 2, col % 2, lax.axis_index("row")
    place = jnp.stack([z, core, row]).astype(jnp.int32)

    mine = panel_rows(matrix, NEAR) | panel_rows(matrix, FAR)
    own = share_panel(mine, z)
    other = swap_cores(own)

    step = 2 * PIECE
    steps = rows // step
    own_spec = pl.BlockSpec((step, BLOCK), lambda g, place: (g, 0))
    panel_spec = pl.BlockSpec((step, FULL), lambda g, place: (g, 0))
    share_rows = SHARE * blocks * width // TILE
    high, low, terms = call(
        product_kernel, "product", 20, (steps,),
        [own_spec, own_spec]
        + [
            pl.BlockSpec((PIECE, blocks, width), lambda g, place, e=e: (lax.rem(place[0] + 2 * g + e, DEPTH), 0, 0))
            for e in range(2)
        ],
        [panel_spec, panel_spec, whole(PEERS, share_rows + TILES * 8, TILE)],
        [bf16(rows, FULL), bf16(rows, FULL), f32(PEERS, share_rows + TILES * 8, TILE)],
        [pltpu.VMEM((FULL, FULL), jnp.float32)],
    )(place, own, other, *in_hbm(matrix, matrix))
    gram_rows = TILES * 8
    gram, sums = call(
        total_kernel, "total", 16, (1,),
        [whole(PEERS, share_rows + gram_rows, TILE)],
        [whole(PEERS, gram_rows, TILE), whole(PEERS, share_rows, TILE)],
        [f32(PEERS, gram_rows, TILE), pltpu.HBM((PEERS, share_rows, TILE), jnp.float32)],
    )(place, exchange(terms))
    gram = exchange(gram)
    sums = exchange(sums)

    m, qh, ql = call(
        factor_kernel, "factor", 20, (1,),
        [whole(PEERS, TILES * 8, TILE)] * 2 + [whole(rows, FULL)] * 2,
        [whole(FULL, FULL), whole(rows, FULL), whole(rows, FULL)],
        [f32(FULL, FULL), bf16(rows, FULL), bf16(rows, FULL)],
        [pltpu.VMEM((NB, FULL, TILE), jnp.float32), pltpu.VMEM((NB, TILE, FULL), jnp.float32)],
    )(place, gram, swap_cores(gram), *in_hbm(high, low))

    a_spec = pl.BlockSpec((step, blocks, width), lambda g, place: (g, 0, 0))
    return call(
        remainder_kernel, "remainder", 22, (steps,),
        [panel_spec, panel_spec, a_spec, whole(FULL, FULL), whole(PEERS, share_rows, TILE)],
        [pl.BlockSpec(memory_space=pl.ANY), a_spec],
        [f32(FULL, blocks, width), f32(rows, blocks, width)],
        [pltpu.VMEM((FULL, blocks * width), jnp.bfloat16)] * 2
        + [pltpu.VMEM((FULL, blocks, width), jnp.float32), pltpu.SemaphoreType.DMA],
    )(place, *in_hbm(qh, ql, matrix), m, sums)


def solution(mesh):
    return jax.shard_map(
        on_device,
        mesh=mesh,
        in_specs=(P("row", None, "col"),),
        out_specs=(P(None, None, "col"), P("row", None, "col")),
        check_vma=False,
    )
```

```python
import jax
import jax.numpy as jnp
from jax import lax
from jax.experimental import pallas as pl
from jax.experimental.pallas import tpu as pltpu
from jax.sharding import PartitionSpec as P

BLOCK = 256
TILE = 128
NB = 4
STRIP = 8
FULL = NB * TILE
PEERS = 16
DEPTH = 8
PIECE = 128
HALF = ((0, 0), (1, 0), (1, 1), (2, 0), (2, 1)), ((2, 2), (3, 0), (3, 1), (3, 2), (3, 3))
HALF_ROWS = len(HALF[0]) * TILE
SHARE = FULL // PEERS
TILES = HALF_ROWS // 8 // PEERS

highest = lax.Precision.HIGHEST
by_rows = ((0,), (0,))
plain = ((1,), (0,))
by_cols = ((1,), (1,))


def mm(a, b, dims):
    return lax.dot_general(a, b, (dims, ((), ())), precision=highest, preferred_element_type=jnp.float32)

def invert_factor(s):
    n = TILE
    rows = lax.broadcasted_iota(jnp.int32, (n, n), 0)
    cols = lax.broadcasted_iota(jnp.int32, (n, n), 1)
    t = jnp.where(rows == cols, 1.0, 0.0).astype(jnp.float32)
    s_done, t_done = [], []
    for k in range(0, n, STRIP):
        top = (k // 8) * 8
        off = k - top
        height = n - top
        sub = lax.broadcasted_iota(jnp.int32, (height, n), 0)
        col = [jnp.broadcast_to(s[:, k + m : k + m + 1], (height, n)) for m in range(STRIP)]
        pivot = [[jnp.broadcast_to(col[j][off + i : off + i + 1, :], (8, n)) for j in range(STRIP)] for i in range(STRIP)]
        srow = [jnp.broadcast_to(s[off + m : off + m + 1, :], (8, n)) for m in range(STRIP)]
        trow = [jnp.broadcast_to(t[off + m : off + m + 1, :], (8, n)) for m in range(STRIP)]
        inv = []
        for m in range(STRIP):
            inv.append(1.0 / pivot[m][m])
            for i in range(m + 1, STRIP):
                low = pivot[i][m] * inv[m]
                for j in range(m + 1, STRIP):
                    if j <= i:
                        pivot[i][j] = pivot[i][j] - low * pivot[j][m]
                srow[i] = srow[i] - low * srow[m]
                trow[i] = trow[i] - low * trow[m]
        def tall(x):
            return jnp.concatenate([x] * (height // 8), axis=0) if height > 8 else x
        factor = []
        for m in range(STRIP):
            f = col[m]
            for j in range(m):
                f = f - factor[j] * tall(pivot[m][j])
            f = f * tall(inv[m])
            factor.append(f)
        for m in range(STRIP):
            f = jnp.where(sub > off + m, factor[m], 0.0)
            s = s - f * tall(srow[m])
            t = t - f * tall(trow[m])
        if off + STRIP == 8:
            s_done.append(s[:8])
            t_done.append(t[:8])
            if height > 8:
                s, t = s[8:], t[8:]
    s = jnp.concatenate(s_done, axis=0)
    t = jnp.concatenate(t_done, axis=0)
    diag = jnp.sum(jnp.where(rows == cols, s, 0.0), axis=1, keepdims=True)
    return t * lax.rsqrt(diag)


def split(x):
    high = x.astype(jnp.bfloat16)
    return high, (x - high.astype(jnp.float32)).astype(jnp.bfloat16)


def one_pass(a, b, dims):
    return lax.dot_general(a, b, (dims, ((), ())), preferred_element_type=jnp.float32)


def three_pass(a, b, dims):
    return one_pass(a[0], b[0], dims) + (one_pass(a[0], b[1], dims) + one_pass(a[1], b[0], dims))


def panel_kernel(matrix_ref, *refs):
    outs, sems = refs[:-1], refs[-1]
    copies = [
        pltpu.make_async_copy(matrix_ref.at[k * PIECE : (k + 1) * PIECE, 0, :], out, sems.at[k]) for k, out in enumerate(outs)
    ]
    for copy in copies:
        copy.start()
    for copy in copies:
        copy.wait()


def product_kernel(place, own_ref, other_ref, a0_ref, a1_ref, high_ref, low_ref, terms_ref, gram_ref):
    start = pl.program_id(0) == 0

    @pl.when(start)
    def _():
        terms_ref[...] = jnp.zeros_like(terms_ref)
        gram_ref[...] = jnp.zeros_like(gram_ref)

    first = place[1] == 0
    own, other = own_ref[...], other_ref[...]
    panel = split(jnp.concatenate([jnp.where(first, own, other), jnp.where(first, other, own)], axis=1))
    high_ref[...], low_ref[...] = panel
    gram_ref[...] += three_pass(panel, panel, by_rows) + one_pass(panel[1], panel[1], by_rows)
    for l in range(a0_ref.shape[1]):
        a = split(jnp.concatenate([a0_ref[:, l, :], a1_ref[:, l, :]], axis=0))
        part = three_pass(panel, a, by_rows)
        for r in range(PEERS):
            for e in range(BLOCK // TILE):
                spot = slice((l * BLOCK // TILE + e) * SHARE, (l * BLOCK // TILE + e + 1) * SHARE)
                terms_ref[r, spot, :] += part[r * SHARE : (r + 1) * SHARE, e * TILE : (e + 1) * TILE]

    @pl.when(pl.program_id(0) == pl.num_programs(0) - 1)
    def _():
        for n in range(HALF_ROWS // 8):
            (i, j), (p, q) = (half[n // 16] for half in HALF)
            top = n % 16 * 8
            here = gram_ref[i * TILE + top : i * TILE + top + 8, j * TILE : (j + 1) * TILE]
            there = gram_ref[p * TILE + top : p * TILE + top + 8, q * TILE : (q + 1) * TILE]
            spot = terms_ref.shape[1] + (n % TILES - TILES) * 8
            terms_ref[n // TILES, spot : spot + 8, :] = jnp.where(first, here, there)


def total_kernel(place, terms_ref, gram_ref, sums_ref):
    peers, split_row = sums_ref.shape[:2]
    total = terms_ref[0]
    for r in range(1, peers):
        total = total + terms_ref[r]
    for r in range(peers):
        sums_ref[r] = total[:split_row]
        gram_ref[r] = total[split_row:]


def factor_kernel(place, own_ref, other_ref, high_ref, low_ref, m_ref, qh_ref, ql_ref, s_ref, t_ref):
    first = place[1] == 0
    s_ref[...] = jnp.zeros_like(s_ref)
    t_ref[...] = jnp.zeros_like(t_ref)
    for n in range(HALF_ROWS // 8):
        (i, j), (p, q) = (half[n // 16] for half in HALF)
        top = n % 16 * 8
        spot = slice(n % TILES * 8, n % TILES * 8 + 8)
        own = own_ref[n // TILES, spot, :]
        other = other_ref[n // TILES, spot, :]
        s_ref[j, i * TILE + top : i * TILE + top + 8, :] = jnp.where(first, own, other)
        s_ref[q, p * TILE + top : p * TILE + top + 8, :] = jnp.where(first, other, own)

    def update(j, i, k):
        s_ref[k, i * TILE : (i + 1) * TILE, :] -= mm(low[i], low[k], by_cols)

    for j in range(NB):
        d = j * TILE
        mj = invert_factor(s_ref[j, d : d + TILE, :])
        if j:
            done = j - 1
            for i in range(j, NB):
                t_ref[i, :, :d] -= three_pass(split(low[i]), split(m_ref[done * TILE : d, :d]), plain)
                for k in range(j, i + 1):
                    if i > j:
                        update(done, i, k)
            m_ref[d : d + TILE, :d] = three_pass(split(mj), split(t_ref[j, :, :d]), plain)
        m_ref[d : d + TILE, d : d + TILE] = mj
        if j + 1 < NB:
            m_ref[d : d + TILE, d + TILE :] = jnp.zeros((TILE, FULL - d - TILE), jnp.float32)
            column = mm(s_ref[j, d + TILE :, :], mj, by_cols)
            low = {i: column[(i - j - 1) * TILE : (i - j) * TILE] for i in range(j + 1, NB)}
            update(j, j + 1, j + 1)

    factor = split(m_ref[...])
    step = 2 * PIECE
    for g in range(0, DEPTH, 2):
        window = slice(g * PIECE, g * PIECE + step)
        q = split(three_pass((high_ref[window], low_ref[window]), factor, by_cols))
        for e in range(2):
            spot = pl.ds(pl.multiple_of(lax.rem(place[0] + g + e, DEPTH) * PIECE, PIECE), PIECE)
            qh_ref[spot, :] = q[0][e * PIECE : (e + 1) * PIECE]
            ql_ref[spot, :] = q[1][e * PIECE : (e + 1) * PIECE]


def remainder_kernel(place, qh_ref, ql_ref, a_ref, m_ref, w_ref, coeff_ref, out_ref, ch_ref, cl_ref, c_ref, sem):
    width = a_ref.shape[2]
    each = width // TILE
    copy = pltpu.make_async_copy(c_ref, coeff_ref, sem)

    @pl.when(pl.program_id(0) == 0)
    def _():
        factor = split(m_ref[...])
        for l in range(c_ref.shape[1]):
            tiles = [w_ref[:, t * SHARE : (t + 1) * SHARE, :].reshape(FULL, TILE) for t in range(l * each, (l + 1) * each)]
            coeffs = three_pass(factor, split(jnp.concatenate(tiles, axis=1)), plain)
            c_ref[:, l, :] = coeffs
            window = slice(l * width, (l + 1) * width)
            ch_ref[:, window], cl_ref[:, window] = split(coeffs)
        copy.start()

    q = qh_ref[...], ql_ref[...]
    for l in range(a_ref.shape[1]):
        window = slice(l * width, (l + 1) * width)
        out_ref[:, l, :] = a_ref[:, l, :] - three_pass(q, (ch_ref[:, window], cl_ref[:, window]), plain)

    @pl.when(pl.program_id(0) == pl.num_programs(0) - 1)
    def _():
        copy.wait()


def call(kernel, name, mib, grid, ins, outs, out_shape, scratch=()):
    return pl.pallas_call(
        kernel,
        out_shape=out_shape,
        grid_spec=pltpu.PrefetchScalarGridSpec(
            num_scalar_prefetch=1, grid=grid, in_specs=ins, out_specs=outs, scratch_shapes=scratch
        ),
        compiler_params=pltpu.CompilerParams(vmem_limit_bytes=mib << 20),
        name=name,
    )


def whole(*shape):
    return pl.BlockSpec(shape, lambda g, place: (0,) * len(shape))


def resident():
    return pl.BlockSpec(memory_space=pltpu.VMEM)


def f32(*shape):
    return jax.ShapeDtypeStruct(shape, jnp.float32)


def bf16(*shape):
    return pltpu.HBM(shape, jnp.bfloat16)


def in_hbm(*arrays):
    return [pltpu.with_memory_space_constraint(x, pltpu.HBM) for x in arrays]


def shift(x, axis, by):
    return lax.ppermute(x, axis, [(i, (i + by) % PEERS) for i in range(PEERS)])


def exchange(x):
    return lax.all_to_all(x, "row", 0, 0)


def swap_cores(x):
    return lax.ppermute(x, "col", [(i, i ^ 1) for i in range(PEERS)])


def share_panel(mine, z):
    own = jnp.where(z == 0, mine[0], jnp.zeros((PIECE, BLOCK), jnp.float32))
    for k in (1, 7, 2, 6, 4, 3, 5):
        own = own + lax.ppermute(mine[k], "col", [(0, 2 * k), (1, 2 * k + 1)])
    own = lax.optimization_barrier(own)
    up, down = [own], [own]
    for _ in range(DEPTH // 2 - 1):
        up.append(shift(up[-1], "col", 2))
        down.append(shift(down[-1], "col", -2))
    half = PIECE // 2
    far = [shift(up[-1][:half], "col", 2), shift(down[-1][half:], "col", -2)]
    return jnp.concatenate(down + far + up[:0:-1], axis=0)


def on_device(matrix):
    rows, blocks, width = matrix.shape
    col = lax.axis_index("col")
    z, core, row = col // 2, col % 2, lax.axis_index("row")
    place = jnp.stack([z, core, row]).astype(jnp.int32)

    mine = pl.pallas_call(
        panel_kernel,
        in_specs=[pl.BlockSpec(memory_space=pl.ANY)],
        out_specs=[pl.BlockSpec(memory_space=pltpu.VMEM)] * DEPTH,
        out_shape=[f32(PIECE, width)] * DEPTH,
        scratch_shapes=[pltpu.SemaphoreType.DMA((DEPTH,))],
        name="panel",
    )(*in_hbm(matrix))
    own = share_panel(mine, z)
    other = swap_cores(own)

    step = 2 * PIECE
    steps = rows // step
    own_spec = pl.BlockSpec((step, BLOCK), lambda g, place: (g, 0))
    panel_spec = pl.BlockSpec((step, FULL), lambda g, place: (g, 0))
    share_rows = SHARE * blocks * width // TILE
    high, low, terms = call(
        product_kernel, "product", 20, (steps,),
        [own_spec, own_spec]
        + [
            pl.BlockSpec((PIECE, blocks, width), lambda g, place, e=e: (lax.rem(place[0] + 2 * g + e, DEPTH), 0, 0))
            for e in range(2)
        ],
        [panel_spec, panel_spec, whole(PEERS, share_rows + TILES * 8, TILE)],
        [bf16(rows, FULL), bf16(rows, FULL), f32(PEERS, share_rows + TILES * 8, TILE)],
        [pltpu.VMEM((FULL, FULL), jnp.float32)],
    )(place, own, other, *in_hbm(matrix, matrix))
    gram_rows = TILES * 8
    gram, sums = call(
        total_kernel, "total", 16, (1,),
        [resident()],
        [whole(PEERS, gram_rows, TILE), whole(PEERS, share_rows, TILE)],
        [f32(PEERS, gram_rows, TILE), pltpu.HBM((PEERS, share_rows, TILE), jnp.float32)],
    )(place, exchange(terms))
    gram = exchange(gram)
    sums = exchange(sums)

    m, qh, ql = call(
        factor_kernel, "factor", 20, (1,),
        [resident()] * 2 + [whole(rows, FULL)] * 2,
        [whole(FULL, FULL), whole(rows, FULL), whole(rows, FULL)],
        [f32(FULL, FULL), bf16(rows, FULL), bf16(rows, FULL)],
        [pltpu.VMEM((NB, FULL, TILE), jnp.float32), pltpu.VMEM((NB, TILE, FULL), jnp.float32)],
    )(place, gram, swap_cores(gram), *in_hbm(high, low))

    a_spec = pl.BlockSpec((step, blocks, width), lambda g, place: (g, 0, 0))
    return call(
        remainder_kernel, "remainder", 22, (steps,),
        [panel_spec, panel_spec, a_spec, resident(), resident()],
        [pl.BlockSpec(memory_space=pl.ANY), a_spec],
        [f32(FULL, blocks, width), f32(rows, blocks, width)],
        [pltpu.VMEM((FULL, blocks * width), jnp.bfloat16)] * 2
        + [pltpu.VMEM((FULL, blocks, width), jnp.float32), pltpu.SemaphoreType.DMA],
    )(place, *in_hbm(qh, ql, matrix), m, sums)


def solution(mesh):
    return jax.shard_map(
        on_device,
        mesh=mesh,
        in_specs=(P("row", None, "col"),),
        out_specs=(P(None, None, "col"), P("row", None, "col")),
        check_vma=False,
    )
```
